128 devices in a mesh: row: 16 (over z, x), col: 8 (over y, core).
Axes of the slice: x: 4, y: 4, z: 4, core: 2. Of those that a mesh axis runs over, the one named last changes fastest.
Arguments:
- child_front: bfloat16 [16, 4096, 1024], P('row', 'col'), may hold values from -6 to 6
- child_inverse: bfloat16 [16, 1024, 1024], P('row'), as said below
- child_index: int32 [16, 32], P('row'), may hold values from 0 to 79, as said below
- child_size: int32 [16], P('row'), may hold values from 4 to 32, as said below
- front: float32 [10240, 10240], P('row', 'col'), may hold values from -6 to 6
- panel_inverse: float32 [256, 256], replicated, as said below
Outputs:
- trailing: float32 [10240, 10240], P('row', 'col')
- panel_rows: float32 [10240, 256], P('row')
The draws below stay inside these ranges and needn't reach their ends.
Inputs may be any that keep to these rules, and one draw needn't show every extreme that they name: `child_index`: for each child r, the entries t < child_size[r] are increasing root tile numbers; later entries are arbitrary tile numbers and are not used. Cutting the root tiles into aligned runs of 5 tiles, a child has at most 2 live tiles in any run, and exactly 2 in each of two neighbouring runs 2q and 2q + 1 for some q. `child_size`: some child has the smallest and some child the largest possible size in every draw. `child_inverse`: lower triangular with a positive diagonal. `panel_inverse`: lower triangular with a positive diagonal.
All inputs are finite; a program needn't handle non-finite values.
Results may differ from the reference program's by a relative error of at most 0.0034.
Values may be sent and summed in bfloat16 or wider, within the bound.
A program may use at most 128 MiB of HBM per device.

```python
import jax
import jax.numpy as jnp
from jax import lax

TILE = 128
TILES = 80
PIV = 1024
PANEL = 256
BLOCK_TILES = 2
ROOT = 10240
CHILDREN = 16
CHILD_TILES = 32


def child_layout(key):
    folded = jax.random.fold_in(key, 7)
    run_tiles = TILES // CHILDREN
    pick_key, top_key, low_key = jax.random.split(folded, 3)
    top_child = jax.random.randint(top_key, (), 0, CHILDREN)
    low_child = (top_child + 1 + jax.random.randint(low_key, (), 0, CHILDREN - 1)) % CHILDREN

    def inverse_order(order_key):
        return jnp.argsort(jax.random.permutation(order_key, run_tiles))

    def one_child(child_id, child_key):
        count_key, order_key, fill_key = jax.random.split(child_key, 3)
        run_ids = jnp.arange(CHILDREN)
        counts = jax.random.randint(count_key, (CHILDREN,), 1, BLOCK_TILES + 1)
        counts = jnp.where(child_id == top_child, BLOCK_TILES, counts)
        counts = jnp.where(child_id == low_child, 0, counts)
        counts = jnp.where(run_ids // 2 == child_id // 2, BLOCK_TILES, counts)
        positions = jax.vmap(inverse_order)(jax.random.split(order_key, CHILDREN))
        chosen = (positions < counts[:, None]).reshape(-1)
        chosen_count = jnp.sum(chosen.astype(jnp.int32))
        listed = jnp.nonzero(chosen, size=CHILD_TILES, fill_value=0)[0].astype(jnp.int32)
        spare_tiles = jax.random.randint(fill_key, (CHILD_TILES,), 0, TILES)
        slot_ids = jnp.arange(CHILD_TILES)
        return (jnp.where(slot_ids < chosen_count, listed, spare_tiles).astype(jnp.int32), chosen_count.astype(jnp.int32))
    return jax.vmap(one_child)(jnp.arange(CHILDREN), jax.random.split(pick_key, CHILDREN))


def draw_child_index(key, part):
    return child_layout(key)[0]


def draw_child_size(key, part):
    return child_layout(key)[1]


def lower_factor(key, count, order, strict_scale, diag_scale):
    normal_key, diag_key = jax.random.split(key)
    entries = jnp.clip(jax.random.normal(normal_key, (count, order, order), jnp.float32), -4.0, 4.0)
    diagonal = jnp.exp(jax.random.uniform(diag_key, (count, order), jnp.float32, jnp.log(0.5), jnp.log(2.0)))
    lower_part = jnp.tril(entries, -1) * strict_scale
    return lower_part + diagonal[:, :, None] * jnp.eye(order, dtype=jnp.float32)[None, :, :] * diag_scale


def draw_child_inverse(key, part):
    result = lower_factor(jax.random.fold_in(key, 11), CHILDREN, PIV, 1.4 * PIV ** (-0.75), PIV ** (-0.25))
    return result.astype(jnp.bfloat16)


def draw_panel_inverse(key, part):
    result = lower_factor(jax.random.fold_in(key, 13), 1, PANEL, 0.5 / (2.0 * PANEL ** 0.5), 1.0 / (2.0 * PANEL ** 0.5))
    return result[0].astype(jnp.float32)


def level_of(own_key, dims, pieces, low, largest):
    def one(position, blocks):
        draws = jax.random.uniform(jax.random.fold_in(jax.random.fold_in(own_key, 6), position), (blocks,), jnp.float32, low / len(pieces), largest / len(pieces))
        return jnp.repeat(jnp.exp(draws), dims[position] // blocks).reshape((-1,) + (1,) * (len(dims) - position - 1))

    factor_of = one(*pieces[0])
    for cut in pieces[1:]:
        factor_of = factor_of * one(*cut)
    return factor_of


def gaussian(own_key, shape, spread, bound, shards=(), kind=jnp.bfloat16):
    factor_of = level_of(own_key, shape, shards, -0.22, 0.18) if shards else 1.0
    values = jax.random.normal(own_key, shape, jnp.float32) * spread * factor_of
    return jnp.minimum(jnp.maximum(values, -bound), bound).astype(kind)


def setup_inputs(seed: int = 0) -> dict:
    streams_of = jax.random.split(jax.random.key(seed), 7)
    child_front = gaussian(streams_of[0], (CHILDREN, CHILD_TILES * TILE, PIV), 1.0, 6.0, ((0, 16), (1, 8)))
    child_inverse = draw_child_inverse(jax.random.fold_in(streams_of[6], 71), 0)
    child_index = draw_child_index(jax.random.fold_in(streams_of[6], 71), 0)
    child_size = draw_child_size(jax.random.fold_in(streams_of[6], 71), 0)
    front = gaussian(streams_of[4], (ROOT, ROOT), 1.0, 6.0, ((0, 16), (1, 8)), jnp.float32)
    panel_inverse = draw_panel_inverse(jax.random.fold_in(streams_of[6], 71), 0)
    return dict(child_front=child_front, child_inverse=child_inverse, child_index=child_index, child_size=child_size, front=front, panel_inverse=panel_inverse)


def reference(child_front, child_inverse, child_index, child_size, front, panel_inverse):
    precise = lax.Precision.HIGHEST
    tiled = front.reshape(TILES, TILE, TILES, TILE)

    def add_child(carried, inputs):
        front_rows, inverse, tile_index, tile_count = inputs
        factor = jnp.dot(front_rows.astype(jnp.float32), inverse.astype(jnp.float32).T, precision=precise).astype(jnp.bfloat16)
        widened = factor.astype(jnp.float32)
        contribution = -jnp.dot(widened, widened.T, precision=precise)
        live_tiles = jnp.arange(CHILD_TILES, dtype=jnp.int32) < tile_count
        targets = jnp.where(live_tiles, tile_index, TILES).astype(jnp.int32)
        contribution_tiles = contribution.reshape(CHILD_TILES, TILE, CHILD_TILES, TILE).transpose(0, 2, 1, 3)
        carried = carried.at[targets[:, None], :, targets[None, :], :].add(contribution_tiles, mode="drop")
        return carried, None

    tiled, ignored = lax.scan(add_child, tiled, (child_front, child_inverse, child_index, child_size))
    assembled = tiled.reshape(ROOT, ROOT)
    panel_rows = jnp.dot(assembled[:, :PANEL], panel_inverse.T, precision=precise)
    trailing = assembled - jnp.dot(panel_rows, panel_rows.T, precision=precise)
    return trailing, panel_rows
```

```python
import functools

import jax
import jax.numpy as jnp
from jax import lax
from jax.experimental import pallas as pl
from jax.experimental.pallas import tpu as pltpu
from jax.sharding import PartitionSpec as P

TILE = 128
PANEL = 256
RUN = 5
SLOTS = 32
PIV = 1024
RUNS = 16
COLS = 8
PART = 512
ROWS = RUN * TILE
PAIR = 2 * TILE
HALF = ROWS // 2
NT = (((1,), (1,)), ((), ()))
BF16 = jnp.bfloat16
F32 = jnp.float32


def tile_rows(index):
    return pl.ds(pl.multiple_of(index * TILE, TILE), TILE)


def exchange_kernel(
    meta_ref, meta_vmem, child_ref, inverse_ref, front_ref, panel_inverse_ref,
    arrived_first, arrived_second, panel_row, panel_col, meta_all,
    factor, column_tiles, outgoing, panel, meta_smem,
    own_send, pass_send, sibling_send, gather_recv,
    block_send, block_recv, meta_send, meta_recv, local_sem,
    row_send, row_recv, col_send, col_recv,
):
    arrived = (arrived_first, arrived_second)
    row = lax.axis_index("row")
    col = lax.axis_index("col")
    z, x = row // 4, row % 4
    y, core = col // 2, col % 2
    up = {"row": row, "col": ((y + 1) % 4) * 2 + core}
    down = {"row": row, "col": ((y + 3) % 4) * 2 + core}
    sibling = {"row": row, "col": y * 2 + 1 - core}

    def peer_row(step):
        return ((z + step // 4) % 4) * 4 + (x + step % 4) % 4

    def peer(step):
        return {"row": peer_row(step), "col": col}

    def remote(src, dst, send, recv, device):
        return pltpu.make_async_remote_copy(
            src_ref=src, dst_ref=dst, send_sem=send, recv_sem=recv,
            device_id=device, device_id_type=pl.DeviceIdType.MESH,
        )

    barrier = pltpu.get_barrier_semaphore()
    for device in (up, down, sibling):
        pl.semaphore_signal(barrier, inc=1, device_id=device, device_id_type=pl.DeviceIdType.MESH)

    @pl.loop(1, RUNS)
    def _(step):
        pl.semaphore_signal(barrier, inc=1, device_id=peer(step), device_id_type=pl.DeviceIdType.MESH)

    panel_in = pltpu.make_async_copy(front_ref.at[:, pl.ds(0, PANEL)], panel, local_sem.at[0])
    panel_in.start()

    def make_own(t):
        part = lax.dot_general(
            child_ref[0, pl.ds(t * TILE, TILE), :], inverse_ref[0], NT, preferred_element_type=F32
        )
        factor[col * 4 + t] = part.astype(BF16)

    for t in range(4):
        make_own(t)

    pl.semaphore_wait(barrier, 3 + RUNS - 1)

    @pl.loop(1, RUNS)
    def _(step):
        remote(meta_vmem, meta_all.at[row], meta_send.at[step], meta_recv.at[row], peer(step)).start()

    meta_own = pltpu.make_async_copy(meta_vmem, meta_all.at[row], local_sem.at[1])
    meta_own.start()

    def part_tile(c, t):
        return factor.at[c * 4 + t]

    def part_copy(c, t, send, device):
        return remote(part_tile(c, t), part_tile(c, t), send, gather_recv.at[c * 4 + t], device)

    below = ((y + 3) % 4) * 2 + core
    above = ((y + 1) % 4) * 2 + core
    across = ((y + 2) % 4) * 2 + core
    sent = []

    def send_part(c, t, send, device):
        copy = part_copy(c, t, send, device)
        copy.start()
        sent.append(copy)

    def recv_part(c, t):
        part_copy(c, t, own_send.at[0, 0], sibling).wait_recv()

    up_order, down_order = (0, 1, 2, 3), (2, 3, 0, 1)
    for a, b in zip(up_order, down_order):
        send_part(col, a, own_send.at[0, a], up)
        send_part(col, b, own_send.at[1, b], down)
    for t in range(4):
        send_part(col, t, sibling_send.at[0, t], sibling)
    for a, b in zip(up_order, down_order):
        recv_part(below, a)
        if a < 2:
            send_part(below, a, pass_send.at[0, a], up)
        send_part(below, a, sibling_send.at[1, a], sibling)
        recv_part(above, b)
        if b >= 2:
            send_part(above, b, pass_send.at[1, b - 2], down)
        send_part(above, b, sibling_send.at[2, b], sibling)
    for t in (0, 2, 1, 3):
        recv_part(across, t)
        send_part(across, t, sibling_send.at[3, t], sibling)
    for chip in range(4):
        for t in range(4):
            recv_part(chip * 2 + 1 - core, t)

    for slot in range(4):
        column_tiles[pl.ds(slot * TILE, TILE), :] = factor[meta_ref[0, col * 4 + slot]]

    def block(half, target):
        first = factor[meta_ref[0, 2 * target]]
        second = factor[meta_ref[0, 2 * target + 1]]
        rows = jnp.concatenate([first, second], axis=0)
        product = lax.dot_general(
            rows, column_tiles[pl.ds(half * PAIR, PAIR), :], NT, preferred_element_type=F32
        )
        return (-product).astype(BF16)

    def put_block(place, value):
        for a in range(2):
            for b in range(2):
                place[a, b] = value[a * TILE:(a + 1) * TILE, b * TILE:(b + 1) * TILE]

    def block_copy(half, step):
        return remote(
            outgoing.at[half, step], arrived[half].at[row],
            block_send.at[half, step], block_recv.at[half, row], peer(step),
        )

    for half in range(2):
        put_block(arrived[half].at[row], block(half, row))

        @pl.loop(1, RUNS)
        def _(step):
            put_block(outgoing.at[half, step], block(half, peer_row(step)))

            @pl.when(step > 1)
            def _():
                block_copy(half, step - 1).start()

        block_copy(half, RUNS - 1).start()

    def wait_blocks(half):
        @pl.loop(1, RUNS)
        def _(step):
            source = peer_row(step)
            remote(
                outgoing.at[half, step], arrived[half].at[source],
                block_send.at[half, step], block_recv.at[half, source], peer(step),
            ).wait_recv()

    meta_own.wait()

    @pl.loop(1, RUNS)
    def _(step):
        source = peer_row(step)
        remote(
            meta_vmem, meta_all.at[source], meta_send.at[step], meta_recv.at[source], peer(step)
        ).wait_recv()

    meta_in = pltpu.make_async_copy(meta_all, meta_smem, local_sem.at[2])
    meta_in.start()
    meta_in.wait()
    panel_in.wait()
    wait_blocks(0)

    def half_rows(h):
        return pl.ds(h * HALF, HALF)

    started = []

    def row_copy(h, kind, device):
        return remote(
            panel_row.at[half_rows(h), :], panel_row.at[half_rows(h), :],
            row_send.at[kind, h], row_recv.at[h], device,
        )

    def recv_row(h):
        row_copy(h, 0, sibling).wait_recv()

    @pl.when(col == 0)
    def _():
        @pl.loop(0, RUNS)
        def _(child):
            for i in range(RUN):
                row_slot = meta_smem[child, 2, RUN * row + i]
                row_here = meta_smem[child, 3, RUN * row + i]
                for j in range(PANEL // TILE):
                    col_slot = meta_smem[child, 2, j]
                    here = row_here * meta_smem[child, 3, j]
                    tile = arrived_first[child, row_slot, col_slot]
                    place = (pl.ds(i * TILE, TILE), pl.ds(j * TILE, TILE))
                    keep = jnp.full((TILE, TILE), here, jnp.int32) != 0
                    panel[place] += jnp.where(keep, tile.astype(F32), 0.0)

        panel_row[...] = lax.dot_general(
            panel[...], panel_inverse_ref[...], NT, precision=lax.Precision.HIGHEST,
            preferred_element_type=F32,
        ).astype(BF16)

    @pl.when(col == 0)
    def _():
        row_copy(0, 0, up).start()
        row_copy(1, 1, down).start()
        row_copy(1, 0, up).start()
        row_copy(0, 1, down).start()
        for h in range(2):
            row_copy(h, 2, sibling).start()

    @pl.when(col == 2)
    def _():
        recv_row(0)
        row_copy(0, 0, up).start()
        row_copy(0, 2, sibling).start()
        recv_row(1)
        row_copy(1, 2, sibling).start()

    @pl.when(col == 6)
    def _():
        recv_row(1)
        row_copy(1, 1, down).start()
        row_copy(1, 2, sibling).start()
        recv_row(0)
        row_copy(0, 2, sibling).start()

    @pl.when(col == 4)
    def _():
        recv_row(0)
        row_copy(0, 2, sibling).start()
        recv_row(1)
        row_copy(1, 2, sibling).start()

    @pl.when(core == 1)
    def _():
        recv_row(0)
        recv_row(1)

    kinds = (peer(4), peer(12), peer(1), peer(3))
    owner_dz = (z + 4 - y) % 4
    mine = (x // 2) == core

    def col_copy(j, h, kind):
        part = panel_col.at[j, half_rows(h), :]
        return remote(part, part, col_send.at[kind, h, j], col_recv.at[j, h], kinds[kind])

    def recv_col(j, h):
        col_copy(j, h, 0).wait_recv()

    @pl.when(mine & (owner_dz == 0))
    def _():
        panel_col[x % 2] = panel_row[...]
        col_copy(x % 2, 0, 0).start()
        col_copy(x % 2, 1, 1).start()
        col_copy(x % 2, 1, 0).start()
        col_copy(x % 2, 0, 1).start()
        col_copy(x % 2, 0, 2).start()
        col_copy(x % 2, 1, 3).start()
        col_copy(x % 2, 1, 2).start()
        col_copy(x % 2, 0, 3).start()

    @pl.when(mine & (owner_dz == 1))
    def _():
        recv_col(x % 2, 0)
        col_copy(x % 2, 0, 0).start()
        col_copy(x % 2, 0, 2).start()
        col_copy(x % 2, 0, 3).start()
        recv_col(x % 2, 1)
        col_copy(x % 2, 1, 2).start()
        col_copy(x % 2, 1, 3).start()

    @pl.when(mine & (owner_dz == 3))
    def _():
        recv_col(x % 2, 1)
        col_copy(x % 2, 1, 1).start()
        col_copy(x % 2, 1, 2).start()
        col_copy(x % 2, 1, 3).start()
        recv_col(x % 2, 0)
        col_copy(x % 2, 0, 2).start()
        col_copy(x % 2, 0, 3).start()

    @pl.when(mine & (owner_dz == 2))
    def _():
        recv_col(x % 2, 0)
        col_copy(x % 2, 0, 2).start()
        col_copy(x % 2, 0, 3).start()
        recv_col(x % 2, 1)
        col_copy(x % 2, 1, 2).start()
        col_copy(x % 2, 1, 3).start()

    for j in range(2):
        dx = (x + 4 - (2 * core + j)) % 4

        @pl.when(dx == 1)
        def _():
            recv_col(j, 0)
            col_copy(j, 0, 2).start()
            recv_col(j, 1)

        @pl.when(dx == 3)
        def _():
            recv_col(j, 1)
            col_copy(j, 1, 3).start()
            recv_col(j, 0)

        @pl.when(dx == 2)
        def _():
            recv_col(j, 0)
            recv_col(j, 1)

    wait_blocks(1)

    for copy in sent:
        copy.wait_send()
    for half in range(2):
        @pl.loop(1, RUNS)
        def _(step):
            block_copy(half, step).wait_send()

    @pl.loop(1, RUNS)
    def _(step):
        remote(meta_vmem, meta_all.at[row], meta_send.at[step], meta_recv.at[row], peer(step)).wait_send()

    for h in range(2):
        @pl.when(core == 0)
        def _():
            row_copy(h, 2, sibling).wait_send()

        @pl.when(col == 0)
        def _():
            row_copy(h, 0, up).wait_send()
            row_copy(h, 1, down).wait_send()

        for kind in (2, 3):
            @pl.when(mine)
            def _():
                col_copy(x % 2, h, kind).wait_send()

        @pl.when(mine & (owner_dz == 0))
        def _():
            col_copy(x % 2, h, 0).wait_send()
            col_copy(x % 2, h, 1).wait_send()

    @pl.when(col == 2)
    def _():
        row_copy(0, 0, up).wait_send()

    @pl.when(col == 6)
    def _():
        row_copy(1, 1, down).wait_send()

    @pl.when(mine & (owner_dz == 1))
    def _():
        col_copy(x % 2, 0, 0).wait_send()

    @pl.when(mine & (owner_dz == 3))
    def _():
        col_copy(x % 2, 1, 1).wait_send()

    for j in range(2):
        dx = (x + 4 - (2 * core + j)) % 4

        @pl.when(dx == 1)
        def _():
            col_copy(j, 0, 2).wait_send()

        @pl.when(dx == 3)
        def _():
            col_copy(j, 1, 3).wait_send()


def exchange(meta, child_front, child_inverse, front, panel_inverse):
    vmem = pl.BlockSpec(memory_space=pltpu.VMEM)
    dma = pltpu.SemaphoreType.DMA
    return pl.pallas_call(
        exchange_kernel,
        out_shape=(
            jax.ShapeDtypeStruct((RUNS, 2, 2, TILE, TILE), BF16),
            jax.ShapeDtypeStruct((RUNS, 2, 2, TILE, TILE), BF16),
            jax.ShapeDtypeStruct((ROWS, PANEL), BF16),
            jax.ShapeDtypeStruct((2, ROWS, PANEL), BF16),
            jax.ShapeDtypeStruct((RUNS, 8, 128), jnp.int32),
        ),
        in_specs=[
            pl.BlockSpec(memory_space=pltpu.SMEM), vmem, vmem, vmem,
            pl.BlockSpec(memory_space=pl.ANY), vmem,
        ],
        out_specs=(vmem, vmem, vmem, vmem, vmem),
        scratch_shapes=[
            pltpu.VMEM((SLOTS, TILE, PIV), BF16),
            pltpu.VMEM((4 * TILE, PIV), BF16),
            pltpu.VMEM((2, RUNS, 2, 2, TILE, TILE), BF16),
            pltpu.VMEM((ROWS, PANEL), F32),
            pltpu.SMEM((RUNS, 8, 128), jnp.int32),
            dma((2, 4)), dma((2, 2)), dma((4, 4)), dma((SLOTS,)),
            dma((2, RUNS)), dma((2, RUNS)), dma((RUNS,)), dma((RUNS,)), dma((3,)),
            dma((3, 2)), dma((2,)), dma((4, 2, 2)), dma((2, 2)),
        ],
        compiler_params=pltpu.CompilerParams(
            collective_id=0, has_side_effects=True, vmem_limit_bytes=56 << 20
        ),
        name="exchange",
    )(meta, meta, child_front, child_inverse, front, panel_inverse)


def finish_kernel(meta_ref, front_ref, arrived_first, arrived_second, panel_row, panel_col, trailing):
    row = lax.axis_index("row")
    col = lax.axis_index("col")
    rows = panel_row[...]
    for half in range(2):
        span = pl.ds(half * ROWS, ROWS)
        trailing[:, span] = front_ref[:, span] - lax.dot_general(
            rows, panel_col[half], NT, preferred_element_type=F32
        )
    for half in range(2):
        @pl.loop(0, RUNS)
        def _(child):
            for a in range(2):
                tile_row = meta_ref[child, 1, 2 * row + a]
                for b in range(2):
                    tile_col = meta_ref[child, 1, 4 * col + 2 * half + b]

                    @pl.when((tile_row >= 0) & (tile_col >= 0))
                    def _():
                        place = (tile_rows(tile_row), tile_rows(half * RUN + tile_col))
                        tile = (arrived_first, arrived_second)[half][child, a, b]
                        trailing[place] += tile.astype(F32)


def finish(meta_all, front, arrived_first, arrived_second, panel_row, panel_col):
    vmem = pl.BlockSpec(memory_space=pltpu.VMEM)
    return pl.pallas_call(
        finish_kernel,
        out_shape=jax.ShapeDtypeStruct(front.shape, F32),
        in_specs=[pl.BlockSpec(memory_space=pltpu.SMEM), vmem, vmem, vmem, vmem, vmem],
        out_specs=vmem,
        compiler_params=pltpu.CompilerParams(vmem_limit_bytes=40 << 20),
        name="finish",
    )(meta_all, front, arrived_first, arrived_second, panel_row, panel_col)


def slot_table(child_index, child_size):
    places = jnp.arange(SLOTS, dtype=jnp.int32)
    tiles = jnp.where(places < child_size[0], child_index[0], RUN * RUNS)
    before = jnp.sum((tiles[None, :] < RUN * (places // 2)[:, None]).astype(jnp.int32), axis=1)
    place = jnp.minimum(before + places % 2, SLOTS - 1)
    picked = jnp.sum(jnp.where(place[:, None] == places[None, :], tiles[None, :], 0), axis=1)
    local = picked - RUN * (places // 2)
    live = (local >= 0) & (local < RUN) & (before + places % 2 < SLOTS)
    wanted = jnp.arange(RUN * RUNS, dtype=jnp.int32)
    match = (picked[None, :] == wanted[:, None]) & live[None, :]
    slot = jnp.sum(jnp.where(match, places % 2, 0), axis=1)
    held = jnp.sum(match.astype(jnp.int32), axis=1)

    def lane(values):
        return jnp.pad(values, (0, 128 - values.shape[0]))

    table = jnp.stack([lane(place), lane(jnp.where(live, local, -1)), lane(slot), lane(held)])
    return jnp.pad(table, ((0, 4), (0, 0)))


def shards(child_front, child_inverse, child_index, child_size, front, panel_inverse):
    meta = slot_table(child_index, child_size)
    arrived_first, arrived_second, panel_row, panel_col, meta_all = exchange(
        meta, child_front, child_inverse, front, panel_inverse
    )
    trailing = finish(meta_all, front, arrived_first, arrived_second, panel_row, panel_col)
    return trailing, panel_row.astype(F32)


def solution(mesh):
    in_specs = (
        P("row", "col", None),
        P("row", None, None),
        P("row", None),
        P("row"),
        P("row", "col"),
        P(),
    )
    out_specs = (P("row", "col"), P("row", None))
    return jax.shard_map(shards, mesh=mesh, in_specs=in_specs, out_specs=out_specs, check_vma=False)
```

```python
import functools

import jax
import jax.numpy as jnp
from jax import lax
from jax.experimental import pallas as pl
from jax.experimental.pallas import tpu as pltpu
from jax.sharding import PartitionSpec as P

TILE = 128
PANEL = 256
RUN = 5
SLOTS = 32
PIV = 1024
RUNS = 16
COLS = 8
PART = 512
ROWS = RUN * TILE
PAIR = 2 * TILE
HALF = ROWS // 2
NT = (((1,), (1,)), ((), ()))
NEAR = (1, 3, 4, 12, 5, 15, 7, 13, 2, 8, 9, 6, 11, 14, 10)
EARLY, MIDDLE = 4, 9
BF16 = jnp.bfloat16
F32 = jnp.float32


def tile_rows(index):
    return pl.ds(pl.multiple_of(index * TILE, TILE), TILE)


def exchange_kernel(
    meta_ref, meta_vmem, child_ref, inverse_hbm, front_ref, panel_inverse_ref,
    arrived_first, arrived_second, panel_row, work, meta_all,
    children, factor, column_tiles, outgoing, panel, panel_col, inverse_ref, meta_smem,
    own_send, pass_send, sibling_send, gather_recv,
    block_send, block_recv, meta_send, meta_recv, local_sem,
    row_send, row_recv, col_send, col_recv,
):
    arrived = (arrived_first, arrived_second)
    row = lax.axis_index("row")
    col = lax.axis_index("col")
    z, x = row // 4, row % 4
    y, core = col // 2, col % 2
    up = {"row": row, "col": ((y + 1) % 4) * 2 + core}
    down = {"row": row, "col": ((y + 3) % 4) * 2 + core}
    sibling = {"row": row, "col": y * 2 + 1 - core}

    def peer_row(step):
        return ((z + step // 4) % 4) * 4 + (x + step % 4) % 4

    def peer(step):
        return {"row": peer_row(step), "col": col}

    def remote(src, dst, send, recv, device):
        return pltpu.make_async_remote_copy(
            src_ref=src, dst_ref=dst, send_sem=send, recv_sem=recv,
            device_id=device, device_id_type=pl.DeviceIdType.MESH,
        )

    barrier = pltpu.get_barrier_semaphore()
    for device in (up, down, sibling):
        pl.semaphore_signal(barrier, inc=1, device_id=device, device_id_type=pl.DeviceIdType.MESH)

    @pl.loop(1, RUNS)
    def _(step):
        pl.semaphore_signal(barrier, inc=1, device_id=peer(step), device_id_type=pl.DeviceIdType.MESH)

    inverse_in = pltpu.make_async_copy(inverse_hbm.at[0], inverse_ref, local_sem.at[2])
    inverse_in.start()
    child_in = pltpu.make_async_copy(child_ref.at[0], children.at[pl.ds(col * 4, 4)], local_sem.at[3])
    child_in.start()
    front_in = pltpu.make_async_copy(front_ref, work, local_sem.at[0])
    front_in.start()
    pl.semaphore_wait(barrier, 3 + RUNS - 1)

    def part_copy(c, t, send, device):
        tile = children.at[c * 4 + t]
        return remote(tile, tile, send, gather_recv.at[c * 4 + t], device)

    below = ((y + 3) % 4) * 2 + core
    above = ((y + 1) % 4) * 2 + core
    across = ((y + 2) % 4) * 2 + core
    sent = []

    def send_part(c, t, send, device, own=False):
        copy = part_copy(c, t, send, device)
        if own:
            copy = remote(
                child_ref.at[0, t], children.at[c * 4 + t], send, gather_recv.at[c * 4 + t], device
            )
        copy.start()
        sent.append(copy)

    def recv_part(c, t):
        part_copy(c, t, own_send.at[0, 0], sibling).wait_recv()

    def make_factor(*tiles):
        rows = jnp.concatenate([children[c * 4 + t] for c, t in tiles], axis=0)
        for j in range(PIV // PAIR):
            depth = (j + 1) * PAIR
            part = lax.dot_general(
                rows[:, :depth], inverse_ref[pl.ds(j * PAIR, PAIR), pl.ds(0, depth)], NT,
                preferred_element_type=F32,
            ).astype(BF16)
            for i, (c, t) in enumerate(tiles):
                factor[c * 4 + t, :, pl.ds(j * PAIR, PAIR)] = part[i * TILE:(i + 1) * TILE]

    up_order, down_order = (0, 1, 2, 3), (2, 3, 0, 1)
    for a, b in zip(up_order, down_order):
        send_part(col, a, own_send.at[0, a], up, own=True)
        send_part(col, b, own_send.at[1, b], down, own=True)
    for t in range(4):
        send_part(col, t, sibling_send.at[0, t], sibling, own=True)

    @pl.loop(1, RUNS)
    def _(step):
        remote(meta_vmem, meta_all.at[row], meta_send.at[step], meta_recv.at[row], peer(step)).start()

    meta_own = pltpu.make_async_copy(meta_vmem, meta_all.at[row], local_sem.at[1])
    meta_own.start()
    child_in.wait()
    inverse_in.wait()
    make_factor((col, 0), (col, 1), (col, 2), (col, 3))
    partner = y * 2 + 1 - core
    for t in range(4):
        recv_part(partner, t)
    make_factor((partner, 0), (partner, 1), (partner, 2), (partner, 3))
    twins = tuple(((y + d) % 4) * 2 + 1 - core for d in (3, 1, 2))
    for a, b in zip(up_order, down_order):
        recv_part(below, a)
        if a < 2:
            send_part(below, a, pass_send.at[0, a], up)
        send_part(below, a, sibling_send.at[1, a], sibling)
        recv_part(above, b)
        if b >= 2:
            send_part(above, b, pass_send.at[1, b - 2], down)
        send_part(above, b, sibling_send.at[2, b], sibling)
        make_factor((below, a), (above, b))
        recv_part(twins[0], a)
        recv_part(twins[1], b)
        make_factor((twins[0], a), (twins[1], b))
    for a, b in ((0, 2), (1, 3)):
        for t in (a, b):
            recv_part(across, t)
            send_part(across, t, sibling_send.at[3, t], sibling)
        make_factor((across, a), (across, b))
        for t in (a, b):
            recv_part(twins[2], t)
        make_factor((twins[2], a), (twins[2], b))

    meta_own.wait()

    @pl.loop(1, RUNS)
    def _(step):
        source = peer_row(step)
        remote(
            meta_vmem, meta_all.at[source], meta_send.at[step], meta_recv.at[source], peer(step)
        ).wait_recv()

    meta_in = pltpu.make_async_copy(meta_all, meta_smem, local_sem.at[1])
    meta_in.start()

    for slot in range(4):
        column_tiles[pl.ds(slot * TILE, TILE), :] = factor[meta_ref[0, col * 4 + slot]]

    def block(half, target):
        first = factor[meta_ref[0, 2 * target]]
        second = factor[meta_ref[0, 2 * target + 1]]
        rows = jnp.concatenate([first, second], axis=0)
        product = lax.dot_general(
            rows, column_tiles[pl.ds(half * PAIR, PAIR), :], NT, preferred_element_type=F32
        )
        return (-product).astype(BF16)

    def put_block(place, value):
        for a in range(2):
            for b in range(2):
                place[a, b] = value[a * TILE:(a + 1) * TILE, b * TILE:(b + 1) * TILE]

    def block_copy(half, step):
        return remote(
            outgoing.at[half, step], arrived[half].at[row],
            block_send.at[half, step], block_recv.at[half, row], peer(step),
        )

    eager = col != 1
    for half in range(2):
        put_block(arrived[half].at[row], block(half, row))
        held = None
        for step in NEAR:
            put_block(outgoing.at[half, step], block(half, peer_row(step)))
            if held is not None:
                @pl.when(eager)
                def _():
                    block_copy(half, held).start()
            held = step if half == 0 or step in NEAR[:EARLY] else None
        if held is not None:
            @pl.when(eager)
            def _():
                block_copy(half, held).start()

    @pl.when(col == 1)
    def _():
        for half in range(2):
            for step in NEAR if half == 0 else NEAR[:EARLY]:
                block_copy(half, step).start()

    def send_late(first, last):
        for step in NEAR[first:last]:
            block_copy(1, step).start()

    def wait_blocks(half):
        @pl.loop(1, RUNS)
        def _(step):
            source = peer_row(step)
            remote(
                outgoing.at[half, step], arrived[half].at[source],
                block_send.at[half, step], block_recv.at[half, source], peer(step),
            ).wait_recv()

    meta_in.wait()
    front_in.wait()
    wait_blocks(0)

    def half_rows(h):
        return pl.ds(h * HALF, HALF)

    def row_copy(h, kind, device):
        return remote(
            panel_row.at[half_rows(h), :], panel_row.at[half_rows(h), :],
            row_send.at[kind, h], row_recv.at[h], device,
        )

    def recv_row(h):
        row_copy(h, 0, sibling).wait_recv()

    @pl.when(col == 0)
    def _():
        for j in range(PANEL // TILE):
            @pl.loop(0, RUN)
            def _(i):
                def add(child, total):
                    tile = arrived_first[
                        child, meta_smem[child, 2, RUN * row + i], meta_smem[child, 2, j]
                    ]
                    here = meta_smem[child, 3, RUN * row + i] * meta_smem[child, 3, j]
                    keep = jnp.full((TILE, TILE), here, jnp.int32) != 0
                    return total + jnp.where(keep, tile.astype(F32), 0.0)

                start = work[tile_rows(i), pl.ds(j * TILE, TILE)]
                panel[tile_rows(i), pl.ds(j * TILE, TILE)] = lax.fori_loop(0, RUNS, add, start, unroll=4)

        for h in range(2):
            panel_row[half_rows(h), :] = lax.dot_general(
                panel[half_rows(h), :], panel_inverse_ref[...], NT, precision=lax.Precision.HIGHEST,
                preferred_element_type=F32,
            ).astype(BF16)

    kinds = (peer(4), peer(12), peer(1), peer(3))
    owner_dz = (z + 4 - y) % 4
    mine = (x // 2) == core

    def col_copy(j, h, kind):
        part = panel_col.at[j, half_rows(h), :]
        return remote(part, part, col_send.at[kind, h, j], col_recv.at[j, h], kinds[kind])

    def source_copy(h, kind):
        return remote(
            panel_row.at[half_rows(h), :], panel_col.at[x % 2, half_rows(h), :],
            col_send.at[kind, h, x % 2], col_recv.at[x % 2, h], kinds[kind],
        )

    def recv_col(j, h):
        col_copy(j, h, 0).wait_recv()

    def row_stage(h):
        @pl.when(col == 0)
        def _():
            row_copy(h, 0, up).start()
            row_copy(h, 1, down).start()

        @pl.when((core == 1) | (y > 0))
        def _():
            recv_row(h)

        if h == 0:
            @pl.when(col == 2)
            def _():
                row_copy(h, 0, up).start()
        else:
            @pl.when(col == 6)
            def _():
                row_copy(h, 1, down).start()

        @pl.when(core == 0)
        def _():
            row_copy(h, 2, sibling).start()

        @pl.when(mine & (owner_dz == 0))
        def _():
            for kind in range(4):
                source_copy(h, kind).start()
            panel_col[x % 2, half_rows(h), :] = panel_row[half_rows(h), :]

    def z_stage(h):
        @pl.when(mine & (owner_dz != 0))
        def _():
            recv_col(x % 2, h)
            if h == 0:
                @pl.when(owner_dz == 1)
                def _():
                    col_copy(x % 2, h, 0).start()
            else:
                @pl.when(owner_dz == 3)
                def _():
                    col_copy(x % 2, h, 1).start()
            col_copy(x % 2, h, 2).start()
            col_copy(x % 2, h, 3).start()

    def x_stage(h):
        for j in range(2):
            dx = (x + 4 - (2 * core + j)) % 4

            @pl.when(dx != 0)
            def _():
                recv_col(j, h)

            @pl.when(dx == (1 if h == 0 else 3))
            def _():
                col_copy(j, h, 2 if h == 0 else 3).start()

    row_stage(0)
    row_stage(1)
    send_late(EARLY, MIDDLE)
    z_stage(0)
    z_stage(1)
    send_late(MIDDLE, RUNS - 1)
    x_stage(0)
    x_stage(1)

    for half in range(2):
        span = pl.ds(half * ROWS, ROWS)
        work[:, span] -= lax.dot_general(
            panel_row[...], panel_col[half], NT, preferred_element_type=F32
        )
    wait_blocks(1)

    for copy in sent:
        copy.wait_send()
    for half in range(2):
        @pl.loop(1, RUNS)
        def _(step):
            block_copy(half, step).wait_send()

    @pl.loop(1, RUNS)
    def _(step):
        remote(meta_vmem, meta_all.at[row], meta_send.at[step], meta_recv.at[row], peer(step)).wait_send()

    for h in range(2):
        @pl.when(core == 0)
        def _():
            row_copy(h, 2, sibling).wait_send()

        @pl.when(col == 0)
        def _():
            row_copy(h, 0, up).wait_send()
            row_copy(h, 1, down).wait_send()

        @pl.when(mine & (owner_dz == 0))
        def _():
            for kind in range(4):
                source_copy(h, kind).wait_send()

        @pl.when(mine & (owner_dz != 0))
        def _():
            col_copy(x % 2, h, 2).wait_send()
            col_copy(x % 2, h, 3).wait_send()

    @pl.when(col == 2)
    def _():
        row_copy(0, 0, up).wait_send()

    @pl.when(col == 6)
    def _():
        row_copy(1, 1, down).wait_send()

    @pl.when(mine & (owner_dz == 1))
    def _():
        col_copy(x % 2, 0, 0).wait_send()

    @pl.when(mine & (owner_dz == 3))
    def _():
        col_copy(x % 2, 1, 1).wait_send()

    for j in range(2):
        dx = (x + 4 - (2 * core + j)) % 4

        @pl.when(dx == 1)
        def _():
            col_copy(j, 0, 2).wait_send()

        @pl.when(dx == 3)
        def _():
            col_copy(j, 1, 3).wait_send()


def exchange(meta, child_front, child_inverse, front, panel_inverse):
    vmem = pl.BlockSpec(memory_space=pltpu.VMEM)
    dma = pltpu.SemaphoreType.DMA
    return pl.pallas_call(
        exchange_kernel,
        out_shape=(
            pltpu.VMEM((RUNS, 2, 2, TILE, TILE), BF16),
            pltpu.VMEM((RUNS, 2, 2, TILE, TILE), BF16),
            pltpu.VMEM((ROWS, PANEL), BF16),
            pltpu.VMEM(front.shape, F32),
            pltpu.VMEM((RUNS, 8, 128), jnp.int32),
        ),
        in_specs=[
            pl.BlockSpec(memory_space=pltpu.SMEM), vmem, pl.BlockSpec(memory_space=pl.ANY),
            pl.BlockSpec(memory_space=pl.ANY), pl.BlockSpec(memory_space=pl.ANY), vmem,
        ],
        out_specs=(vmem, vmem, vmem, vmem, vmem),
        scratch_shapes=[
            pltpu.VMEM((SLOTS, TILE, PIV), BF16),
            pltpu.VMEM((SLOTS, TILE, PIV), BF16),
            pltpu.VMEM((4 * TILE, PIV), BF16),
            pltpu.VMEM((2, RUNS, 2, 2, TILE, TILE), BF16),
            pltpu.VMEM((ROWS, PANEL), F32),
            pltpu.VMEM((2, ROWS, PANEL), BF16),
            pltpu.VMEM((PIV, PIV), BF16),
            pltpu.SMEM((RUNS, 8, 128), jnp.int32),
            dma((2, 4)), dma((2, 2)), dma((4, 4)), dma((SLOTS,)),
            dma((2, RUNS)), dma((2, RUNS)), dma((RUNS,)), dma((RUNS,)), dma((4,)),
            dma((3, 2)), dma((2,)), dma((4, 2, 2)), dma((2, 2)),
        ],
        compiler_params=pltpu.CompilerParams(
            collective_id=0, has_side_effects=True, vmem_limit_bytes=48 << 20
        ),
        name="exchange",
    )(meta, meta, child_front.reshape(1, PART // TILE, TILE, PIV), child_inverse, front, panel_inverse)


def finish_kernel(
    meta_ref, work, arrived_first, arrived_second, panel_row, trailing, panel_out, result, out_sem
):
    row = lax.axis_index("row")
    col = lax.axis_index("col")
    stores = []
    for half, arrived in enumerate((arrived_first, arrived_second)):
        span = pl.ds(half * ROWS, ROWS)
        result[:, span] = work[:, span]

        @pl.loop(0, RUNS)
        def _(child):
            for a in range(2):
                tile_row = meta_ref[child, 1, 2 * row + a]
                for b in range(2):
                    tile_col = meta_ref[child, 1, 4 * col + 2 * half + b]

                    @pl.when((tile_row >= 0) & (tile_col >= 0))
                    def _():
                        place = (tile_rows(tile_row), tile_rows(half * RUN + tile_col))
                        result[place] += arrived[child, a, b].astype(F32)

        store = pltpu.make_async_copy(result.at[:, span], trailing.at[:, span], out_sem.at[half])
        store.start()
        stores.append(store)
    panel_out[...] = panel_row[...].astype(F32)
    for store in stores:
        store.wait()


def finish(meta_all, work, arrived_first, arrived_second, panel_row):
    vmem = pl.BlockSpec(memory_space=pltpu.VMEM)
    return pl.pallas_call(
        finish_kernel,
        out_shape=(
            jax.ShapeDtypeStruct(work.shape, F32), jax.ShapeDtypeStruct((ROWS, PANEL), F32)
        ),
        in_specs=[pl.BlockSpec(memory_space=pltpu.SMEM), vmem, vmem, vmem, vmem],
        out_specs=(pl.BlockSpec(memory_space=pl.ANY), vmem),
        scratch_shapes=[
            pltpu.VMEM(work.shape, F32), pltpu.SemaphoreType.DMA((2,)),
        ],
        compiler_params=pltpu.CompilerParams(vmem_limit_bytes=16 << 20),
        name="finish",
    )(meta_all, work, arrived_first, arrived_second, panel_row)


def slot_table(child_index, child_size):
    places = jnp.arange(SLOTS, dtype=jnp.int32)
    tiles = jnp.where(places < child_size[0], child_index[0], RUN * RUNS)
    before = jnp.sum((tiles[None, :] < RUN * (places // 2)[:, None]).astype(jnp.int32), axis=1)
    place = jnp.minimum(before + places % 2, SLOTS - 1)
    picked = jnp.sum(jnp.where(place[:, None] == places[None, :], tiles[None, :], 0), axis=1)
    local = picked - RUN * (places // 2)
    live = (local >= 0) & (local < RUN) & (before + places % 2 < SLOTS)
    wanted = jnp.arange(RUN * RUNS, dtype=jnp.int32)
    match = (picked[None, :] == wanted[:, None]) & live[None, :]
    slot = jnp.sum(jnp.where(match, places % 2, 0), axis=1)
    held = jnp.sum(match.astype(jnp.int32), axis=1)

    def lane(values):
        return jnp.pad(values, (0, 128 - values.shape[0]))

    table = jnp.stack([lane(place), lane(jnp.where(live, local, -1)), lane(slot), lane(held)])
    return jnp.pad(table, ((0, 4), (0, 0)))


def shards(child_front, child_inverse, child_index, child_size, front, panel_inverse):
    meta = slot_table(child_index, child_size)
    arrived_first, arrived_second, panel_row, work, meta_all = exchange(
        meta, child_front, child_inverse, front, panel_inverse
    )
    return finish(meta_all, work, arrived_first, arrived_second, panel_row)


def solution(mesh):
    in_specs = (
        P("row", "col", None),
        P("row", None, None),
        P("row", None),
        P("row"),
        P("row", "col"),
        P(),
    )
    out_specs = (P("row", "col"), P("row", None))
    return jax.shard_map(shards, mesh=mesh, in_specs=in_specs, out_specs=out_specs, check_vma=False)
```

```python
import functools

import jax
import jax.numpy as jnp
from jax import lax
from jax.experimental import pallas as pl
from jax.experimental.pallas import tpu as pltpu
from jax.sharding import PartitionSpec as P

TILE = 128
PANEL = 256
RUN = 5
SLOTS = 32
PIV = 1024
RUNS = 16
COLS = 8
PART = 512
ROWS = RUN * TILE
PAIR = 2 * TILE
HALF = ROWS // 2
NT = (((1,), (1,)), ((), ()))
NEAR = (1, 3, 4, 12, 5, 15, 7, 13, 2, 8, 9, 6, 11, 14, 10)
BF16 = jnp.bfloat16
F32 = jnp.float32


def tile_rows(index):
    return pl.ds(pl.multiple_of(index * TILE, TILE), TILE)


def exchange_kernel(
    meta_ref, meta_vmem, child_ref, inverse_hbm, front_ref, panel_inverse_ref,
    arrived_first, arrived_second, panel_row, work, meta_all,
    children, factor, column_tiles, outgoing, panel, panel_col, inverse_ref, meta_smem,
    own_send, pass_send, sibling_send, gather_recv,
    block_send, block_recv, meta_send, meta_recv, local_sem,
    row_send, row_recv, col_send, col_recv,
):
    arrived = (arrived_first, arrived_second)
    row = lax.axis_index("row")
    col = lax.axis_index("col")
    z, x = row // 4, row % 4
    y, core = col // 2, col % 2
    up = {"row": row, "col": ((y + 1) % 4) * 2 + core}
    down = {"row": row, "col": ((y + 3) % 4) * 2 + core}
    sibling = {"row": row, "col": y * 2 + 1 - core}
    opposite = {"row": row, "col": ((y + 2) % 4) * 2 + core}

    def peer_row(step):
        return ((z + step // 4) % 4) * 4 + (x + step % 4) % 4

    def peer(step):
        return {"row": peer_row(step), "col": col}

    def remote(src, dst, send, recv, device):
        return pltpu.make_async_remote_copy(
            src_ref=src, dst_ref=dst, send_sem=send, recv_sem=recv,
            device_id=device, device_id_type=pl.DeviceIdType.MESH,
        )

    barrier = pltpu.get_barrier_semaphore()
    for device in (up, down, sibling, opposite):
        pl.semaphore_signal(barrier, inc=1, device_id=device, device_id_type=pl.DeviceIdType.MESH)

    @pl.loop(1, RUNS)
    def _(step):
        pl.semaphore_signal(barrier, inc=1, device_id=peer(step), device_id_type=pl.DeviceIdType.MESH)

    inverse_in = pltpu.make_async_copy(inverse_hbm.at[0], inverse_ref, local_sem.at[2])
    inverse_in.start()
    child_in = pltpu.make_async_copy(child_ref.at[0], children.at[pl.ds(col * 4, 4)], local_sem.at[3])
    child_in.start()
    front_in = pltpu.make_async_copy(front_ref, work, local_sem.at[0])
    front_in.start()
    pl.semaphore_wait(barrier, 4 + RUNS - 1)

    def part_copy(c, t, send, device):
        tile = children.at[c * 4 + t]
        return remote(tile, tile, send, gather_recv.at[c * 4 + t], device)

    below = ((y + 3) % 4) * 2 + core
    above = ((y + 1) % 4) * 2 + core
    across = ((y + 2) % 4) * 2 + core
    sent = []

    def send_part(c, t, send, device, own=False):
        copy = part_copy(c, t, send, device)
        if own:
            copy = remote(
                child_ref.at[0, t], children.at[c * 4 + t], send, gather_recv.at[c * 4 + t], device
            )
        copy.start()
        sent.append(copy)

    def recv_part(c, t):
        part_copy(c, t, own_send.at[0, 0], sibling).wait_recv()

    def make_factor(*tiles):
        rows = jnp.concatenate([children[c * 4 + t] for c, t in tiles], axis=0)
        for j in range(PIV // PAIR):
            depth = (j + 1) * PAIR
            part = lax.dot_general(
                rows[:, :depth], inverse_ref[pl.ds(j * PAIR, PAIR), pl.ds(0, depth)], NT,
                preferred_element_type=F32,
            ).astype(BF16)
            for i, (c, t) in enumerate(tiles):
                factor[c * 4 + t, :, pl.ds(j * PAIR, PAIR)] = part[i * TILE:(i + 1) * TILE]

    up_order, down_order = (0, 1, 2, 3), (2, 3, 0, 1)
    for a, b in zip(up_order, down_order):
        send_part(col, a, own_send.at[0, a], up, own=True)
        send_part(col, b, own_send.at[1, b], down, own=True)
    for t in range(4):
        send_part(col, t, sibling_send.at[0, t], sibling, own=True)

    @pl.loop(1, RUNS)
    def _(step):
        remote(meta_vmem, meta_all.at[row], meta_send.at[step], meta_recv.at[row], peer(step)).start()

    meta_own = pltpu.make_async_copy(meta_vmem, meta_all.at[row], local_sem.at[1])
    meta_own.start()
    child_in.wait()
    inverse_in.wait()
    make_factor((col, 0), (col, 1), (col, 2), (col, 3))
    partner = y * 2 + 1 - core
    for t in range(4):
        recv_part(partner, t)
    make_factor((partner, 0), (partner, 1), (partner, 2), (partner, 3))
    twins = tuple(((y + d) % 4) * 2 + 1 - core for d in (3, 1, 2))
    for a, b in zip(up_order, down_order):
        recv_part(below, a)
        if a < 2:
            send_part(below, a, pass_send.at[0, a], up)
        send_part(below, a, sibling_send.at[1, a], sibling)
        recv_part(above, b)
        if b >= 2:
            send_part(above, b, pass_send.at[1, b - 2], down)
        send_part(above, b, sibling_send.at[2, b], sibling)
        make_factor((below, a), (above, b))
        recv_part(twins[0], a)
        recv_part(twins[1], b)
        make_factor((twins[0], a), (twins[1], b))
    for a, b in ((0, 2), (1, 3)):
        for t in (a, b):
            recv_part(across, t)
            send_part(across, t, sibling_send.at[3, t], sibling)
        make_factor((across, a), (across, b))
        for t in (a, b):
            recv_part(twins[2], t)
        make_factor((twins[2], a), (twins[2], b))

    meta_own.wait()

    @pl.loop(1, RUNS)
    def _(step):
        source = peer_row(step)
        remote(
            meta_vmem, meta_all.at[source], meta_send.at[step], meta_recv.at[source], peer(step)
        ).wait_recv()

    meta_in = pltpu.make_async_copy(meta_all, meta_smem, local_sem.at[1])
    meta_in.start()

    for slot in range(4):
        column_tiles[pl.ds(slot * TILE, TILE), :] = factor[meta_ref[0, col * 4 + slot]]

    def block(half, target):
        first = factor[meta_ref[0, 2 * target]]
        second = factor[meta_ref[0, 2 * target + 1]]
        rows = jnp.concatenate([first, second], axis=0)
        product = lax.dot_general(
            rows, column_tiles[pl.ds(half * PAIR, PAIR), :], NT, preferred_element_type=F32
        )
        return (-product).astype(BF16)

    def put_block(place, value):
        for a in range(2):
            for b in range(2):
                place[a, b] = value[a * TILE:(a + 1) * TILE, b * TILE:(b + 1) * TILE]

    def block_copy(half, step):
        return remote(
            outgoing.at[half, step], arrived[half].at[row],
            block_send.at[half, step], block_recv.at[half, row], peer(step),
        )

    eager = col != 1
    for half in range(2):
        put_block(arrived[half].at[row], block(half, row))
        held = None
        for step in NEAR:
            put_block(outgoing.at[half, step], block(half, peer_row(step)))
            if held is not None:
                @pl.when(eager)
                def _():
                    block_copy(half, held).start()
            held = step
        @pl.when(eager)
        def _():
            block_copy(half, held).start()

    @pl.when(col == 1)
    def _():
        for half in range(2):
            for step in NEAR:
                block_copy(half, step).start()

    def wait_block(half, step):
        source = peer_row(step)
        remote(
            outgoing.at[half, step], arrived[half].at[source],
            block_send.at[half, step], block_recv.at[half, source], peer(step),
        ).wait_recv()

    def wait_blocks(half):
        @pl.loop(1, RUNS)
        def _(step):
            wait_block(half, step)

    meta_in.wait()
    front_in.wait()

    def half_rows(h):
        return pl.ds(h * HALF, HALF)

    def row_copy(h, kind, device):
        return remote(
            panel_row.at[half_rows(h), :], panel_row.at[half_rows(h), :],
            row_send.at[kind, h], row_recv.at[h], device,
        )

    def recv_row(h):
        row_copy(h, 0, sibling).wait_recv()

    wait_blocks(0)

    @pl.when(col == 0)
    def _():
        for j in range(PANEL // TILE):
            @pl.loop(0, RUN)
            def _(i):
                place = (tile_rows(i), pl.ds(j * TILE, TILE))
                total = work[place]
                for child in range(RUNS):
                    tile = arrived_first[
                        child, meta_smem[child, 2, RUN * row + i], meta_smem[child, 2, j]
                    ]
                    here = meta_smem[child, 3, RUN * row + i] * meta_smem[child, 3, j]
                    keep = jnp.full((TILE, TILE), here, jnp.int32) != 0
                    total += jnp.where(keep, tile.astype(F32), 0.0)
                panel[place] = total

        for h in range(2):
            panel_row[half_rows(h), :] = lax.dot_general(
                panel[half_rows(h), :], panel_inverse_ref[...], NT, precision=lax.Precision.HIGHEST,
                preferred_element_type=F32,
            ).astype(BF16)

    kinds = (peer(4), peer(12), peer(8), peer(1), peer(3), peer(2))
    owner_dz = (z + 4 - y) % 4
    mine = (x // 2) == core

    def col_copy(j, h, kind):
        part = panel_col.at[j, half_rows(h), :]
        return remote(part, part, col_send.at[kind, h, j], col_recv.at[j, h], kinds[kind])

    def source_copy(h, kind):
        return remote(
            panel_row.at[half_rows(h), :], panel_col.at[x % 2, half_rows(h), :],
            col_send.at[kind, h, x % 2], col_recv.at[x % 2, h], kinds[kind],
        )

    def recv_col(j, h):
        col_copy(j, h, 0).wait_recv()

    def row_stage(h):
        @pl.when(col == 0)
        def _():
            row_copy(h, 0, up).start()
            row_copy(h, 1, down).start()
            row_copy(h, 2, opposite).start()

        @pl.when((core == 1) | (y > 0))
        def _():
            recv_row(h)

        @pl.when(core == 0)
        def _():
            row_copy(h, 3, sibling).start()

        @pl.when(mine & (owner_dz == 0))
        def _():
            for kind in range(6):
                source_copy(h, kind).start()
            panel_col[x % 2, half_rows(h), :] = panel_row[half_rows(h), :]

    def z_stage(h):
        @pl.when(mine & (owner_dz != 0))
        def _():
            recv_col(x % 2, h)
            for kind in range(3, 6):
                col_copy(x % 2, h, kind).start()

    def x_stage(h):
        for j in range(2):
            @pl.when((x + 4 - (2 * core + j)) % 4 != 0)
            def _():
                recv_col(j, h)

    row_stage(0)
    row_stage(1)
    z_stage(0)
    z_stage(1)
    x_stage(0)
    x_stage(1)

    for half in range(2):
        span = pl.ds(half * ROWS, ROWS)
        work[:, span] -= lax.dot_general(
            panel_row[...], panel_col[half], NT, preferred_element_type=F32
        )
    wait_blocks(1)

    for copy in sent:
        copy.wait_send()
    for half in range(2):
        @pl.loop(1, RUNS)
        def _(step):
            block_copy(half, step).wait_send()

    @pl.loop(1, RUNS)
    def _(step):
        remote(meta_vmem, meta_all.at[row], meta_send.at[step], meta_recv.at[row], peer(step)).wait_send()

    for h in range(2):
        @pl.when(core == 0)
        def _():
            row_copy(h, 3, sibling).wait_send()

        @pl.when(col == 0)
        def _():
            row_copy(h, 0, up).wait_send()
            row_copy(h, 1, down).wait_send()
            row_copy(h, 2, opposite).wait_send()

        @pl.when(mine & (owner_dz == 0))
        def _():
            for kind in range(6):
                source_copy(h, kind).wait_send()

        @pl.when(mine & (owner_dz != 0))
        def _():
            for kind in range(3, 6):
                col_copy(x % 2, h, kind).wait_send()


def exchange(meta, child_front, child_inverse, front, panel_inverse):
    vmem = pl.BlockSpec(memory_space=pltpu.VMEM)
    dma = pltpu.SemaphoreType.DMA
    return pl.pallas_call(
        exchange_kernel,
        out_shape=(
            pltpu.VMEM((RUNS, 2, 2, TILE, TILE), BF16),
            pltpu.VMEM((RUNS, 2, 2, TILE, TILE), BF16),
            pltpu.VMEM((ROWS, PANEL), BF16),
            pltpu.VMEM(front.shape, F32),
            pltpu.VMEM((RUNS, 8, 128), jnp.int32),
        ),
        in_specs=[
            pl.BlockSpec(memory_space=pltpu.SMEM), vmem, pl.BlockSpec(memory_space=pl.ANY),
            pl.BlockSpec(memory_space=pl.ANY), pl.BlockSpec(memory_space=pl.ANY), vmem,
        ],
        out_specs=(vmem, vmem, vmem, vmem, vmem),
        scratch_shapes=[
            pltpu.VMEM((SLOTS, TILE, PIV), BF16),
            pltpu.VMEM((SLOTS, TILE, PIV), BF16),
            pltpu.VMEM((4 * TILE, PIV), BF16),
            pltpu.VMEM((2, RUNS, 2, 2, TILE, TILE), BF16),
            pltpu.VMEM((ROWS, PANEL), F32),
            pltpu.VMEM((2, ROWS, PANEL), BF16),
            pltpu.VMEM((PIV, PIV), BF16),
            pltpu.SMEM((RUNS, 8, 128), jnp.int32),
            dma((2, 4)), dma((2, 2)), dma((4, 4)), dma((SLOTS,)),
            dma((2, RUNS)), dma((2, RUNS)), dma((RUNS,)), dma((RUNS,)), dma((4,)),
            dma((4, 2)), dma((2,)), dma((6, 2, 2)), dma((2, 2)),
        ],
        compiler_params=pltpu.CompilerParams(
            collective_id=0, has_side_effects=True, vmem_limit_bytes=48 << 20
        ),
        name="exchange",
    )(meta, meta, child_front.reshape(1, PART // TILE, TILE, PIV), child_inverse, front, panel_inverse)


def finish_kernel(
    meta_ref, work, arrived_first, arrived_second, panel_row, trailing, panel_out, result, out_sem
):
    row = lax.axis_index("row")
    col = lax.axis_index("col")
    stores = []
    for half, arrived in enumerate((arrived_first, arrived_second)):
        span = pl.ds(half * ROWS, ROWS)
        result[:, span] = work[:, span]

        @pl.loop(0, RUNS)
        def _(child):
            for a in range(2):
                tile_row = meta_ref[child, 1, 2 * row + a]
                for b in range(2):
                    tile_col = meta_ref[child, 1, 4 * col + 2 * half + b]

                    @pl.when((tile_row >= 0) & (tile_col >= 0))
                    def _():
                        place = (tile_rows(tile_row), tile_rows(half * RUN + tile_col))
                        result[place] += arrived[child, a, b].astype(F32)

        store = pltpu.make_async_copy(result.at[:, span], trailing.at[:, span], out_sem.at[half])
        store.start()
        stores.append(store)
    panel_out[...] = panel_row[...].astype(F32)
    for store in stores:
        store.wait()


def finish(meta_all, work, arrived_first, arrived_second, panel_row):
    vmem = pl.BlockSpec(memory_space=pltpu.VMEM)
    return pl.pallas_call(
        finish_kernel,
        out_shape=(
            jax.ShapeDtypeStruct(work.shape, F32), jax.ShapeDtypeStruct((ROWS, PANEL), F32)
        ),
        in_specs=[pl.BlockSpec(memory_space=pltpu.SMEM), vmem, vmem, vmem, vmem],
        out_specs=(pl.BlockSpec(memory_space=pl.ANY), vmem),
        scratch_shapes=[
            pltpu.VMEM(work.shape, F32), pltpu.SemaphoreType.DMA((2,)),
        ],
        compiler_params=pltpu.CompilerParams(vmem_limit_bytes=16 << 20),
        name="finish",
    )(meta_all, work, arrived_first, arrived_second, panel_row)


def slot_table(child_index, child_size):
    places = jnp.arange(SLOTS, dtype=jnp.int32)
    tiles = jnp.where(places < child_size[0], child_index[0], RUN * RUNS)
    before = jnp.sum((tiles[None, :] < RUN * (places // 2)[:, None]).astype(jnp.int32), axis=1)
    place = jnp.minimum(before + places % 2, SLOTS - 1)
    picked = jnp.sum(jnp.where(place[:, None] == places[None, :], tiles[None, :], 0), axis=1)
    local = picked - RUN * (places // 2)
    live = (local >= 0) & (local < RUN) & (before + places % 2 < SLOTS)
    wanted = jnp.arange(RUN * RUNS, dtype=jnp.int32)
    match = (picked[None, :] == wanted[:, None]) & live[None, :]
    slot = jnp.sum(jnp.where(match, places % 2, 0), axis=1)
    held = jnp.sum(match.astype(jnp.int32), axis=1)

    def lane(values):
        return jnp.pad(values, (0, 128 - values.shape[0]))

    table = jnp.stack([lane(place), lane(jnp.where(live, local, -1)), lane(slot), lane(held)])
    return jnp.pad(table, ((0, 4), (0, 0)))


def shards(child_front, child_inverse, child_index, child_size, front, panel_inverse):
    meta = slot_table(child_index, child_size)
    arrived_first, arrived_second, panel_row, work, meta_all = exchange(
        meta, child_front, child_inverse, front, panel_inverse
    )
    return finish(meta_all, work, arrived_first, arrived_second, panel_row)


def solution(mesh):
    in_specs = (
        P("row", "col", None),
        P("row", None, None),
        P("row", None),
        P("row"),
        P("row", "col"),
        P(),
    )
    out_specs = (P("row", "col"), P("row", None))
    return jax.shard_map(shards, mesh=mesh, in_specs=in_specs, out_specs=out_specs, check_vma=False)
```

```python
import functools

import jax
import jax.numpy as jnp
from jax import lax
from jax.experimental import pallas as pl
from jax.experimental.pallas import tpu as pltpu
from jax.sharding import PartitionSpec as P

TILE = 128
PANEL = 256
RUN = 5
SLOTS = 32
PIV = 1024
RUNS = 16
COLS = 8
PART = 512
ROWS = RUN * TILE
PAIR = 2 * TILE
HALF = ROWS // 2
NT = (((1,), (1,)), ((), ()))
NEAR = (1, 3, 4, 12, 5, 15, 7, 13, 2, 8, 9, 6, 11, 14, 10)
BF16 = jnp.bfloat16
F32 = jnp.float32


def tile_rows(index):
    return pl.ds(pl.multiple_of(index * TILE, TILE), TILE)


def slot_table(size_ref, index_ref, index_row, table):
    index_row[...] = jnp.zeros_like(index_row)
    index_row[0:1, 0:SLOTS] = index_ref[...]
    lane = lax.broadcasted_iota(jnp.int32, (1, 128), 1)
    tiles = jnp.where(lane < size_ref[0], index_row[0:1, :], RUN * RUNS)
    tiles = jnp.transpose(jnp.broadcast_to(tiles, (128, 128)))[:SLOTS]
    places = lax.broadcasted_iota(jnp.int32, (SLOTS, 128), 0)

    def total(kept, values):
        return jnp.sum(jnp.where(kept, values, 0), axis=0, keepdims=True)

    one = jnp.ones_like(tiles)
    first = RUN * (lane >> 1)
    order = total(tiles < first, one) + (lane & 1)
    place = jnp.minimum(order, SLOTS - 1)
    local = total(places == place, tiles) - first
    live = (local >= 0) & (local < RUN) & (order < SLOTS)
    same = tiles == lane
    run_first = RUN * ((lane * 205) >> 10)
    held = total(same, one)
    slot = total(same, places) - total(tiles < run_first, one)
    slot = jnp.minimum(jnp.maximum(jnp.where(held > 0, slot, 0), 0), 1)
    for i, values in enumerate((place, jnp.where(live, local, -1), slot, held)):
        table[i:i + 1, :] = values


def exchange_kernel(
    size_ref, index_ref, child_ref, inverse_hbm, front_ref, panel_inverse_ref,
    arrived_first, arrived_second, panel_row, work, meta_all,
    children, factor, column_tiles, outgoing, panel, panel_col, inverse_ref, meta_smem, index_row, meta_vmem,
    own_send, pass_send, sibling_send, gather_recv,
    block_send, block_recv, meta_send, meta_recv, local_sem,
    row_send, row_recv, col_send, col_recv,
):
    arrived = (arrived_first, arrived_second)
    row = lax.axis_index("row")
    col = lax.axis_index("col")
    z, x = row // 4, row % 4
    y, core = col // 2, col % 2
    up = {"row": row, "col": ((y + 1) % 4) * 2 + core}
    down = {"row": row, "col": ((y + 3) % 4) * 2 + core}
    sibling = {"row": row, "col": y * 2 + 1 - core}
    opposite = {"row": row, "col": ((y + 2) % 4) * 2 + core}

    def peer_row(step):
        return ((z + step // 4) % 4) * 4 + (x + step % 4) % 4

    def peer(step):
        return {"row": peer_row(step), "col": col}

    def remote(src, dst, send, recv, device):
        return pltpu.make_async_remote_copy(
            src_ref=src, dst_ref=dst, send_sem=send, recv_sem=recv,
            device_id=device, device_id_type=pl.DeviceIdType.MESH,
        )

    barrier = pltpu.get_barrier_semaphore()
    for device in (up, down, sibling, opposite):
        pl.semaphore_signal(barrier, inc=1, device_id=device, device_id_type=pl.DeviceIdType.MESH)

    @pl.loop(1, RUNS)
    def _(step):
        pl.semaphore_signal(barrier, inc=1, device_id=peer(step), device_id_type=pl.DeviceIdType.MESH)

    inverse_in = pltpu.make_async_copy(inverse_hbm.at[0], inverse_ref, local_sem.at[2])
    inverse_in.start()
    child_in = pltpu.make_async_copy(child_ref.at[0], children.at[pl.ds(col * 4, 4)], local_sem.at[3])
    child_in.start()
    front_in = pltpu.make_async_copy(front_ref, work, local_sem.at[0])
    front_in.start()
    slot_table(size_ref, index_ref, index_row, meta_vmem)
    pl.semaphore_wait(barrier, 4 + RUNS - 1)

    def part_copy(c, t, send, device):
        tile = children.at[c * 4 + t]
        return remote(tile, tile, send, gather_recv.at[c * 4 + t], device)

    below = ((y + 3) % 4) * 2 + core
    above = ((y + 1) % 4) * 2 + core
    across = ((y + 2) % 4) * 2 + core
    sent = []

    def send_part(c, t, send, device, own=False):
        copy = part_copy(c, t, send, device)
        if own:
            copy = remote(
                child_ref.at[0, t], children.at[c * 4 + t], send, gather_recv.at[c * 4 + t], device
            )
        copy.start()
        sent.append(copy)

    def recv_part(c, t):
        part_copy(c, t, own_send.at[0, 0], sibling).wait_recv()

    def make_factor(*tiles):
        rows = jnp.concatenate([children[c * 4 + t] for c, t in tiles], axis=0)
        for j in range(PIV // PAIR):
            depth = (j + 1) * PAIR
            part = lax.dot_general(
                rows[:, :depth], inverse_ref[pl.ds(j * PAIR, PAIR), pl.ds(0, depth)], NT,
                preferred_element_type=F32,
            ).astype(BF16)
            for i, (c, t) in enumerate(tiles):
                factor[c * 4 + t, :, pl.ds(j * PAIR, PAIR)] = part[i * TILE:(i + 1) * TILE]

    up_order, down_order = (0, 1, 2, 3), (2, 3, 0, 1)
    for a, b in zip(up_order, down_order):
        send_part(col, a, own_send.at[0, a], up, own=True)
        send_part(col, b, own_send.at[1, b], down, own=True)
    for t in range(4):
        send_part(col, t, sibling_send.at[0, t], sibling, own=True)

    @pl.loop(1, RUNS)
    def _(step):
        remote(meta_vmem, meta_all.at[row], meta_send.at[step], meta_recv.at[row], peer(step)).start()

    meta_own = pltpu.make_async_copy(meta_vmem, meta_all.at[row], local_sem.at[1])
    meta_own.start()
    child_in.wait()
    inverse_in.wait()
    make_factor((col, 0), (col, 1), (col, 2), (col, 3))
    partner = y * 2 + 1 - core
    for t in range(4):
        recv_part(partner, t)
    make_factor((partner, 0), (partner, 1), (partner, 2), (partner, 3))
    twins = tuple(((y + d) % 4) * 2 + 1 - core for d in (3, 1, 2))
    for a, b in zip(up_order, down_order):
        recv_part(below, a)
        if a < 2:
            send_part(below, a, pass_send.at[0, a], up)
        send_part(below, a, sibling_send.at[1, a], sibling)
        recv_part(above, b)
        if b >= 2:
            send_part(above, b, pass_send.at[1, b - 2], down)
        send_part(above, b, sibling_send.at[2, b], sibling)
        make_factor((below, a), (above, b))
        recv_part(twins[0], a)
        recv_part(twins[1], b)
        make_factor((twins[0], a), (twins[1], b))
    meta_own.wait()

    @pl.loop(1, RUNS)
    def _(step):
        source = peer_row(step)
        remote(
            meta_vmem, meta_all.at[source], meta_send.at[step], meta_recv.at[source], peer(step)
        ).wait_recv()

    meta_in = pltpu.make_async_copy(meta_all, meta_smem, local_sem.at[1])
    meta_in.start()

    for a, b in ((0, 2), (1, 3)):
        for t in (a, b):
            recv_part(across, t)
            send_part(across, t, sibling_send.at[3, t], sibling)
        make_factor((across, a), (across, b))
        for t in (a, b):
            recv_part(twins[2], t)
        make_factor((twins[2], a), (twins[2], b))

    meta_in.wait()

    for slot in range(4):
        column_tiles[pl.ds(slot * TILE, TILE), :] = factor[meta_smem[row, 0, col * 4 + slot]]

    def block(half, target):
        first = factor[meta_smem[row, 0, 2 * target]]
        second = factor[meta_smem[row, 0, 2 * target + 1]]
        rows = jnp.concatenate([first, second], axis=0)
        product = lax.dot_general(
            rows, column_tiles[pl.ds(half * PAIR, PAIR), :], NT, preferred_element_type=F32
        )
        return (-product).astype(BF16)

    def put_block(place, value):
        for a in range(2):
            for b in range(2):
                place[a, b] = value[a * TILE:(a + 1) * TILE, b * TILE:(b + 1) * TILE]

    def block_copy(half, step):
        return remote(
            outgoing.at[half, step], arrived[half].at[row],
            block_send.at[half, step], block_recv.at[half, row], peer(step),
        )

    eager = col != 1
    for half in range(2):
        put_block(arrived[half].at[row], block(half, row))
        held = None
        for step in NEAR:
            put_block(outgoing.at[half, step], block(half, peer_row(step)))
            if held is not None:
                @pl.when(eager)
                def _():
                    block_copy(half, held).start()
            held = step
        @pl.when(eager)
        def _():
            block_copy(half, held).start()

    @pl.when(col == 1)
    def _():
        for half in range(2):
            for step in NEAR:
                block_copy(half, step).start()

    def wait_block(half, step):
        source = peer_row(step)
        remote(
            outgoing.at[half, step], arrived[half].at[source],
            block_send.at[half, step], block_recv.at[half, source], peer(step),
        ).wait_recv()

    def wait_blocks(half):
        @pl.loop(1, RUNS)
        def _(step):
            wait_block(half, step)

    front_in.wait()

    def half_rows(h):
        return pl.ds(h * HALF, HALF)

    def row_copy(h, kind, device):
        return remote(
            panel_row.at[half_rows(h), :], panel_row.at[half_rows(h), :],
            row_send.at[kind, h], row_recv.at[h], device,
        )

    def recv_row(h):
        row_copy(h, 0, sibling).wait_recv()

    wait_blocks(0)

    @pl.when(col == 0)
    def _():
        for j in range(PANEL // TILE):
            @pl.loop(0, RUN)
            def _(i):
                place = (tile_rows(i), pl.ds(j * TILE, TILE))
                total = work[place]
                for child in range(RUNS):
                    tile = arrived_first[
                        child, meta_smem[child, 2, RUN * row + i], meta_smem[child, 2, j]
                    ]
                    here = meta_smem[child, 3, RUN * row + i] * meta_smem[child, 3, j]
                    keep = jnp.full((TILE, TILE), here, jnp.int32) != 0
                    total += jnp.where(keep, tile.astype(F32), 0.0)
                panel[place] = total

        for h in range(2):
            panel_row[half_rows(h), :] = lax.dot_general(
                panel[half_rows(h), :], panel_inverse_ref[...], NT, precision=lax.Precision.HIGHEST,
                preferred_element_type=F32,
            ).astype(BF16)

    kinds = (peer(4), peer(12), peer(8), peer(1), peer(3), peer(2))
    owner_dz = (z + 4 - y) % 4
    mine = (x // 2) == core

    def col_copy(j, h, kind):
        part = panel_col.at[j, half_rows(h), :]
        return remote(part, part, col_send.at[kind, h, j], col_recv.at[j, h], kinds[kind])

    def source_copy(h, kind):
        return remote(
            panel_row.at[half_rows(h), :], panel_col.at[x % 2, half_rows(h), :],
            col_send.at[kind, h, x % 2], col_recv.at[x % 2, h], kinds[kind],
        )

    def recv_col(j, h):
        col_copy(j, h, 0).wait_recv()

    def row_stage(h):
        @pl.when(col == 0)
        def _():
            row_copy(h, 0, up).start()
            row_copy(h, 1, down).start()
            row_copy(h, 2, opposite).start()

        @pl.when((core == 1) | (y > 0))
        def _():
            recv_row(h)

        @pl.when(core == 0)
        def _():
            row_copy(h, 3, sibling).start()

        @pl.when(mine & (owner_dz == 0))
        def _():
            for kind in range(6):
                source_copy(h, kind).start()
            panel_col[x % 2, half_rows(h), :] = panel_row[half_rows(h), :]

    def z_stage(h):
        @pl.when(mine & (owner_dz != 0))
        def _():
            recv_col(x % 2, h)
            for kind in range(3, 6):
                col_copy(x % 2, h, kind).start()

    def x_stage(h):
        for j in range(2):
            @pl.when((x + 4 - (2 * core + j)) % 4 != 0)
            def _():
                recv_col(j, h)

    row_stage(0)
    row_stage(1)
    z_stage(0)
    z_stage(1)
    x_stage(0)
    x_stage(1)

    for half in range(2):
        span = pl.ds(half * ROWS, ROWS)
        work[:, span] -= lax.dot_general(
            panel_row[...], panel_col[half], NT, preferred_element_type=F32
        )
    wait_blocks(1)

    for copy in sent:
        copy.wait_send()
    for half in range(2):
        @pl.loop(1, RUNS)
        def _(step):
            block_copy(half, step).wait_send()

    @pl.loop(1, RUNS)
    def _(step):
        remote(meta_vmem, meta_all.at[row], meta_send.at[step], meta_recv.at[row], peer(step)).wait_send()

    for h in range(2):
        @pl.when(core == 0)
        def _():
            row_copy(h, 3, sibling).wait_send()

        @pl.when(col == 0)
        def _():
            row_copy(h, 0, up).wait_send()
            row_copy(h, 1, down).wait_send()
            row_copy(h, 2, opposite).wait_send()

        @pl.when(mine & (owner_dz == 0))
        def _():
            for kind in range(6):
                source_copy(h, kind).wait_send()

        @pl.when(mine & (owner_dz != 0))
        def _():
            for kind in range(3, 6):
                col_copy(x % 2, h, kind).wait_send()


def exchange(child_size, child_index, child_front, child_inverse, front, panel_inverse):
    vmem = pl.BlockSpec(memory_space=pltpu.VMEM)
    dma = pltpu.SemaphoreType.DMA
    return pl.pallas_call(
        exchange_kernel,
        out_shape=(
            pltpu.VMEM((RUNS, 2, 2, TILE, TILE), BF16),
            pltpu.VMEM((RUNS, 2, 2, TILE, TILE), BF16),
            pltpu.VMEM((ROWS, PANEL), BF16),
            pltpu.VMEM(front.shape, F32),
            pltpu.VMEM((RUNS, 4, 128), jnp.int32),
        ),
        in_specs=[
            pl.BlockSpec(memory_space=pltpu.SMEM), vmem, pl.BlockSpec(memory_space=pl.ANY),
            pl.BlockSpec(memory_space=pl.ANY), pl.BlockSpec(memory_space=pl.ANY), vmem,
        ],
        out_specs=(vmem, vmem, vmem, vmem, vmem),
        scratch_shapes=[
            pltpu.VMEM((SLOTS, TILE, PIV), BF16),
            pltpu.VMEM((SLOTS, TILE, PIV), BF16),
            pltpu.VMEM((4 * TILE, PIV), BF16),
            pltpu.VMEM((2, RUNS, 2, 2, TILE, TILE), BF16),
            pltpu.VMEM((ROWS, PANEL), F32),
            pltpu.VMEM((2, ROWS, PANEL), BF16),
            pltpu.VMEM((PIV, PIV), BF16),
            pltpu.SMEM((RUNS, 4, 128), jnp.int32),
            pltpu.VMEM((8, 128), jnp.int32),
            pltpu.VMEM((4, 128), jnp.int32),
            dma((2, 4)), dma((2, 2)), dma((4, 4)), dma((SLOTS,)),
            dma((2, RUNS)), dma((2, RUNS)), dma((RUNS,)), dma((RUNS,)), dma((4,)),
            dma((4, 2)), dma((2,)), dma((6, 2, 2)), dma((2, 2)),
        ],
        compiler_params=pltpu.CompilerParams(
            collective_id=0, has_side_effects=True, vmem_limit_bytes=48 << 20
        ),
        name="exchange",
    )(child_size, child_index, child_front.reshape(1, PART // TILE, TILE, PIV), child_inverse, front, panel_inverse)


def finish_kernel(
    meta_ref, work, arrived_first, arrived_second, panel_row, trailing, panel_out, result, out_sem
):
    row = lax.axis_index("row")
    col = lax.axis_index("col")
    stores = []
    for half, arrived in enumerate((arrived_first, arrived_second)):
        span = pl.ds(half * ROWS, ROWS)
        result[:, span] = work[:, span]

        @pl.loop(0, RUNS)
        def _(child):
            for a in range(2):
                tile_row = meta_ref[child, 1, 2 * row + a]
                for b in range(2):
                    tile_col = meta_ref[child, 1, 4 * col + 2 * half + b]

                    @pl.when((tile_row >= 0) & (tile_col >= 0))
                    def _():
                        place = (tile_rows(tile_row), tile_rows(half * RUN + tile_col))
                        result[place] += arrived[child, a, b].astype(F32)

        store = pltpu.make_async_copy(result.at[:, span], trailing.at[:, span], out_sem.at[half])
        store.start()
        stores.append(store)
    panel_out[...] = panel_row[...].astype(F32)
    for store in stores:
        store.wait()


def finish(meta_all, work, arrived_first, arrived_second, panel_row):
    vmem = pl.BlockSpec(memory_space=pltpu.VMEM)
    return pl.pallas_call(
        finish_kernel,
        out_shape=(
            jax.ShapeDtypeStruct(work.shape, F32), jax.ShapeDtypeStruct((ROWS, PANEL), F32)
        ),
        in_specs=[pl.BlockSpec(memory_space=pltpu.SMEM), vmem, vmem, vmem, vmem],
        out_specs=(pl.BlockSpec(memory_space=pl.ANY), vmem),
        scratch_shapes=[
            pltpu.VMEM(work.shape, F32), pltpu.SemaphoreType.DMA((2,)),
        ],
        compiler_params=pltpu.CompilerParams(vmem_limit_bytes=16 << 20),
        name="finish",
    )(meta_all, work, arrived_first, arrived_second, panel_row)


def shards(child_front, child_inverse, child_index, child_size, front, panel_inverse):
    arrived_first, arrived_second, panel_row, work, meta_all = exchange(
        child_size, child_index, child_front, child_inverse, front, panel_inverse
    )
    return finish(meta_all, work, arrived_first, arrived_second, panel_row)


def solution(mesh):
    in_specs = (
        P("row", "col", None),
        P("row", None, None),
        P("row", None),
        P("row"),
        P("row", "col"),
        P(),
    )
    out_specs = (P("row", "col"), P("row", None))
    return jax.shard_map(shards, mesh=mesh, in_specs=in_specs, out_specs=out_specs, check_vma=False)
```

```python
import functools

import jax
import jax.numpy as jnp
from jax import lax
from jax.experimental import pallas as pl
from jax.experimental.pallas import tpu as pltpu
from jax.sharding import PartitionSpec as P

TILE = 128
PANEL = 256
RUN = 5
SLOTS = 32
PIV = 1024
RUNS = 16
COLS = 8
PART = 512
ROWS = RUN * TILE
PAIR = 2 * TILE
HALF = ROWS // 4
NT = (((1,), (1,)), ((), ()))
NEAR = (1, 3, 4, 12, 5, 15, 7, 13, 2, 8, 9, 6, 11, 14, 10)
BF16 = jnp.bfloat16
F32 = jnp.float32


def tile_rows(index):
    return pl.ds(pl.multiple_of(index * TILE, TILE), TILE)


def slot_table(size_ref, index_ref, index_row, table):
    index_row[...] = jnp.zeros_like(index_row)
    index_row[0:1, 0:SLOTS] = index_ref[...]
    lane = lax.broadcasted_iota(jnp.int32, (1, 128), 1)
    tiles = jnp.where(lane < size_ref[0], index_row[0:1, :], RUN * RUNS)
    tiles = jnp.transpose(jnp.broadcast_to(tiles, (128, 128)))[:SLOTS]
    places = lax.broadcasted_iota(jnp.int32, (SLOTS, 128), 0)

    def total(kept, values):
        return jnp.sum(jnp.where(kept, values, 0), axis=0, keepdims=True)

    one = jnp.ones_like(tiles)
    first = RUN * (lane >> 1)
    order = total(tiles < first, one) + (lane & 1)
    place = jnp.minimum(order, SLOTS - 1)
    local = total(places == place, tiles) - first
    live = (local >= 0) & (local < RUN) & (order < SLOTS)
    same = tiles == lane
    run_first = RUN * ((lane * 205) >> 10)
    held = total(same, one)
    slot = total(same, places) - total(tiles < run_first, one)
    slot = jnp.minimum(jnp.maximum(jnp.where(held > 0, slot, 0), 0), 1)
    for i, values in enumerate((place, jnp.where(live, local, -1), slot, held)):
        table[i:i + 1, :] = values


def exchange_kernel(
    size_ref, index_ref, child_ref, inverse_hbm, front_ref, panel_inverse_ref,
    arrived_first, arrived_second, panel_row, work, meta_all,
    children, factor, column_tiles, outgoing, panel, panel_col, inverse_ref, meta_smem, index_row, meta_vmem,
    own_send, pass_send, sibling_send, gather_recv,
    block_send, block_recv, meta_send, meta_recv, local_sem,
    row_send, row_recv, col_send, col_recv,
):
    arrived = (arrived_first, arrived_second)
    row = lax.axis_index("row")
    col = lax.axis_index("col")
    z, x = row // 4, row % 4
    y, core = col // 2, col % 2
    up = {"row": row, "col": ((y + 1) % 4) * 2 + core}
    down = {"row": row, "col": ((y + 3) % 4) * 2 + core}
    sibling = {"row": row, "col": y * 2 + 1 - core}
    opposite = {"row": row, "col": ((y + 2) % 4) * 2 + core}

    def peer_row(step):
        return ((z + step // 4) % 4) * 4 + (x + step % 4) % 4

    def peer(step):
        return {"row": peer_row(step), "col": col}

    def remote(src, dst, send, recv, device):
        return pltpu.make_async_remote_copy(
            src_ref=src, dst_ref=dst, send_sem=send, recv_sem=recv,
            device_id=device, device_id_type=pl.DeviceIdType.MESH,
        )

    barrier = pltpu.get_barrier_semaphore()
    for device in (up, down, sibling, opposite):
        pl.semaphore_signal(barrier, inc=1, device_id=device, device_id_type=pl.DeviceIdType.MESH)

    @pl.loop(1, RUNS)
    def _(step):
        pl.semaphore_signal(barrier, inc=1, device_id=peer(step), device_id_type=pl.DeviceIdType.MESH)

    inverse_in = pltpu.make_async_copy(inverse_hbm.at[0], inverse_ref, local_sem.at[2])
    inverse_in.start()
    child_in = pltpu.make_async_copy(child_ref.at[0], children.at[pl.ds(col * 4, 4)], local_sem.at[3])
    child_in.start()
    front_in = pltpu.make_async_copy(front_ref, work, local_sem.at[0])
    front_in.start()
    slot_table(size_ref, index_ref, index_row, meta_vmem)
    pl.semaphore_wait(barrier, 4 + RUNS - 1)

    def part_copy(c, t, send, device):
        tile = children.at[c * 4 + t]
        return remote(tile, tile, send, gather_recv.at[c * 4 + t], device)

    below = ((y + 3) % 4) * 2 + core
    above = ((y + 1) % 4) * 2 + core
    across = ((y + 2) % 4) * 2 + core
    sent = []

    def send_part(c, t, send, device, own=False):
        copy = part_copy(c, t, send, device)
        if own:
            copy = remote(
                child_ref.at[0, t], children.at[c * 4 + t], send, gather_recv.at[c * 4 + t], device
            )
        copy.start()
        sent.append(copy)

    def recv_part(c, t):
        part_copy(c, t, own_send.at[0, 0], sibling).wait_recv()

    def make_factor(*tiles):
        rows = jnp.concatenate([children[c * 4 + t] for c, t in tiles], axis=0)
        for j in range(PIV // PAIR):
            depth = (j + 1) * PAIR
            part = lax.dot_general(
                rows[:, :depth], inverse_ref[pl.ds(j * PAIR, PAIR), pl.ds(0, depth)], NT,
                preferred_element_type=F32,
            ).astype(BF16)
            for i, (c, t) in enumerate(tiles):
                factor[c * 4 + t, :, pl.ds(j * PAIR, PAIR)] = part[i * TILE:(i + 1) * TILE]

    up_order, down_order = (0, 1, 2, 3), (2, 3, 0, 1)
    for a, b in zip(up_order, down_order):
        send_part(col, a, own_send.at[0, a], up, own=True)
        send_part(col, b, own_send.at[1, b], down, own=True)
    for t in range(4):
        send_part(col, t, sibling_send.at[0, t], sibling, own=True)

    @pl.loop(1, RUNS)
    def _(step):
        remote(meta_vmem, meta_all.at[row], meta_send.at[step], meta_recv.at[row], peer(step)).start()

    meta_own = pltpu.make_async_copy(meta_vmem, meta_all.at[row], local_sem.at[1])
    meta_own.start()
    child_in.wait()
    inverse_in.wait()
    make_factor((col, 0), (col, 1), (col, 2), (col, 3))
    partner = y * 2 + 1 - core
    for t in range(4):
        recv_part(partner, t)
    make_factor((partner, 0), (partner, 1), (partner, 2), (partner, 3))
    twins = tuple(((y + d) % 4) * 2 + 1 - core for d in (3, 1, 2))
    for a, b in zip(up_order, down_order):
        recv_part(below, a)
        if a < 2:
            send_part(below, a, pass_send.at[0, a], up)
        send_part(below, a, sibling_send.at[1, a], sibling)
        recv_part(above, b)
        if b >= 2:
            send_part(above, b, pass_send.at[1, b - 2], down)
        send_part(above, b, sibling_send.at[2, b], sibling)
        make_factor((below, a), (above, b))
        recv_part(twins[0], a)
        recv_part(twins[1], b)
        make_factor((twins[0], a), (twins[1], b))
    meta_own.wait()

    @pl.loop(1, RUNS)
    def _(step):
        source = peer_row(step)
        remote(
            meta_vmem, meta_all.at[source], meta_send.at[step], meta_recv.at[source], peer(step)
        ).wait_recv()

    meta_in = pltpu.make_async_copy(meta_all, meta_smem, local_sem.at[1])
    meta_in.start()

    for a, b in ((0, 2), (1, 3)):
        for t in (a, b):
            recv_part(across, t)
            send_part(across, t, sibling_send.at[3, t], sibling)
        make_factor((across, a), (across, b))
        for t in (a, b):
            recv_part(twins[2], t)
        make_factor((twins[2], a), (twins[2], b))

    meta_in.wait()

    for slot in range(4):
        column_tiles[pl.ds(slot * TILE, TILE), :] = factor[meta_smem[row, 0, col * 4 + slot]]

    def block(half, target):
        first = factor[meta_smem[row, 0, 2 * target]]
        second = factor[meta_smem[row, 0, 2 * target + 1]]
        rows = jnp.concatenate([first, second], axis=0)
        product = lax.dot_general(
            rows, column_tiles[pl.ds(half * PAIR, PAIR), :], NT, preferred_element_type=F32
        )
        return (-product).astype(BF16)

    def put_block(place, value):
        for a in range(2):
            for b in range(2):
                place[a, b] = value[a * TILE:(a + 1) * TILE, b * TILE:(b + 1) * TILE]

    def block_copy(half, step):
        return remote(
            outgoing.at[half, step], arrived[half].at[row],
            block_send.at[half, step], block_recv.at[half, row], peer(step),
        )

    eager = col != 1
    for half in range(2):
        put_block(arrived[half].at[row], block(half, row))
        held = None
        for step in NEAR:
            put_block(outgoing.at[half, step], block(half, peer_row(step)))
            if held is not None:
                @pl.when(eager)
                def _():
                    block_copy(half, held).start()
            held = step
        @pl.when(eager)
        def _():
            block_copy(half, held).start()

    @pl.when(col == 1)
    def _():
        for half in range(2):
            for step in NEAR:
                block_copy(half, step).start()

    def wait_block(half, step):
        source = peer_row(step)
        remote(
            outgoing.at[half, step], arrived[half].at[source],
            block_send.at[half, step], block_recv.at[half, source], peer(step),
        ).wait_recv()

    def wait_blocks(half):
        @pl.loop(1, RUNS)
        def _(step):
            wait_block(half, step)

    front_in.wait()

    def half_rows(h):
        return pl.ds(h * HALF, HALF)

    def row_copy(h, kind, device):
        return remote(
            panel_row.at[half_rows(h), :], panel_row.at[half_rows(h), :],
            row_send.at[kind, h], row_recv.at[h], device,
        )

    def recv_row(h):
        row_copy(h, 0, sibling).wait_recv()

    wait_blocks(0)

    @pl.when(col == 0)
    def _():
        for j in range(PANEL // TILE):
            @pl.loop(0, RUN)
            def _(i):
                place = (tile_rows(i), pl.ds(j * TILE, TILE))
                total = work[place]
                for child in range(RUNS):
                    tile = arrived_first[
                        child, meta_smem[child, 2, RUN * row + i], meta_smem[child, 2, j]
                    ]
                    here = meta_smem[child, 3, RUN * row + i] * meta_smem[child, 3, j]
                    keep = jnp.full((TILE, TILE), here, jnp.int32) != 0
                    total += jnp.where(keep, tile.astype(F32), 0.0)
                panel[place] = total

        for h in range(4):
            panel_row[half_rows(h), :] = lax.dot_general(
                panel[half_rows(h), :], panel_inverse_ref[...], NT, precision=lax.Precision.HIGHEST,
                preferred_element_type=F32,
            ).astype(BF16)

    kinds = (peer(4), peer(12), peer(8), peer(1), peer(3), peer(2))
    owner_dz = (z + 4 - y) % 4
    mine = (x // 2) == core

    def col_copy(j, h, kind):
        part = panel_col.at[j, half_rows(h), :]
        return remote(part, part, col_send.at[kind, h, j], col_recv.at[j, h], kinds[kind])

    def source_copy(h, kind):
        return remote(
            panel_row.at[half_rows(h), :], panel_col.at[x % 2, half_rows(h), :],
            col_send.at[kind, h, x % 2], col_recv.at[x % 2, h], kinds[kind],
        )

    def recv_col(j, h):
        col_copy(j, h, 0).wait_recv()

    def row_stage(h):
        @pl.when(col == 0)
        def _():
            row_copy(h, 0, up).start()
            row_copy(h, 1, down).start()
            row_copy(h, 2, opposite).start()

        @pl.when((core == 1) | (y > 0))
        def _():
            recv_row(h)

        @pl.when(core == 0)
        def _():
            row_copy(h, 3, sibling).start()

        @pl.when(mine & (owner_dz == 0))
        def _():
            for kind in range(6):
                source_copy(h, kind).start()
            panel_col[x % 2, half_rows(h), :] = panel_row[half_rows(h), :]

    def z_stage(h):
        @pl.when(mine & (owner_dz != 0))
        def _():
            recv_col(x % 2, h)
            for kind in range(3, 6):
                col_copy(x % 2, h, kind).start()

    for h in range(4):
        row_stage(h)
    for h in range(4):
        z_stage(h)
    for j in (x % 2, 1 - x % 2):
        @pl.when(x != 2 * core + j)
        def _():
            for h in range(4):
                recv_col(j, h)

        span = pl.ds(pl.multiple_of(j * ROWS, TILE), ROWS)
        work[:, span] -= lax.dot_general(
            panel_row[...], panel_col[j], NT, preferred_element_type=F32
        )

    wait_blocks(1)

    for copy in sent:
        copy.wait_send()
    for half in range(2):
        @pl.loop(1, RUNS)
        def _(step):
            block_copy(half, step).wait_send()

    @pl.loop(1, RUNS)
    def _(step):
        remote(meta_vmem, meta_all.at[row], meta_send.at[step], meta_recv.at[row], peer(step)).wait_send()

    for h in range(4):
        @pl.when(core == 0)
        def _():
            row_copy(h, 3, sibling).wait_send()

        @pl.when(col == 0)
        def _():
            row_copy(h, 0, up).wait_send()
            row_copy(h, 1, down).wait_send()
            row_copy(h, 2, opposite).wait_send()

        @pl.when(mine & (owner_dz == 0))
        def _():
            for kind in range(6):
                source_copy(h, kind).wait_send()

        @pl.when(mine & (owner_dz != 0))
        def _():
            for kind in range(3, 6):
                col_copy(x % 2, h, kind).wait_send()


def exchange(child_size, child_index, child_front, child_inverse, front, panel_inverse):
    vmem = pl.BlockSpec(memory_space=pltpu.VMEM)
    dma = pltpu.SemaphoreType.DMA
    return pl.pallas_call(
        exchange_kernel,
        out_shape=(
            pltpu.VMEM((RUNS, 2, 2, TILE, TILE), BF16),
            pltpu.VMEM((RUNS, 2, 2, TILE, TILE), BF16),
            pltpu.VMEM((ROWS, PANEL), BF16),
            pltpu.VMEM(front.shape, F32),
            pltpu.VMEM((RUNS, 4, 128), jnp.int32),
        ),
        in_specs=[
            pl.BlockSpec(memory_space=pltpu.SMEM), vmem, pl.BlockSpec(memory_space=pl.ANY),
            pl.BlockSpec(memory_space=pl.ANY), pl.BlockSpec(memory_space=pl.ANY), vmem,
        ],
        out_specs=(vmem, vmem, vmem, vmem, vmem),
        scratch_shapes=[
            pltpu.VMEM((SLOTS, TILE, PIV), BF16),
            pltpu.VMEM((SLOTS, TILE, PIV), BF16),
            pltpu.VMEM((4 * TILE, PIV), BF16),
            pltpu.VMEM((2, RUNS, 2, 2, TILE, TILE), BF16),
            pltpu.VMEM((ROWS, PANEL), F32),
            pltpu.VMEM((2, ROWS, PANEL), BF16),
            pltpu.VMEM((PIV, PIV), BF16),
            pltpu.SMEM((RUNS, 4, 128), jnp.int32),
            pltpu.VMEM((8, 128), jnp.int32),
            pltpu.VMEM((4, 128), jnp.int32),
            dma((2, 4)), dma((2, 2)), dma((4, 4)), dma((SLOTS,)),
            dma((2, RUNS)), dma((2, RUNS)), dma((RUNS,)), dma((RUNS,)), dma((4,)),
            dma((4, 4)), dma((4,)), dma((6, 4, 2)), dma((2, 4)),
        ],
        compiler_params=pltpu.CompilerParams(
            collective_id=0, has_side_effects=True, vmem_limit_bytes=48 << 20
        ),
        name="exchange",
    )(child_size, child_index, child_front.reshape(1, PART // TILE, TILE, PIV), child_inverse, front, panel_inverse)


def finish_kernel(
    meta_ref, work, arrived_first, arrived_second, panel_row, trailing, panel_out, result, out_sem
):
    row = lax.axis_index("row")
    col = lax.axis_index("col")
    stores = []
    for half, arrived in enumerate((arrived_first, arrived_second)):
        span = pl.ds(half * ROWS, ROWS)
        result[:, span] = work[:, span]

        @pl.loop(0, RUNS)
        def _(child):
            for a in range(2):
                tile_row = meta_ref[child, 1, 2 * row + a]
                for b in range(2):
                    tile_col = meta_ref[child, 1, 4 * col + 2 * half + b]
                    live = (tile_row >= 0) & (tile_col >= 0)
                    keep = jnp.full((TILE, TILE), live.astype(jnp.int32), jnp.int32) != 0
                    place = (
                        tile_rows(jnp.maximum(tile_row, 0)),
                        tile_rows(half * RUN + jnp.maximum(tile_col, 0)),
                    )
                    result[place] += jnp.where(keep, arrived[child, a, b].astype(F32), 0.0)

        store = pltpu.make_async_copy(result.at[:, span], trailing.at[:, span], out_sem.at[half])
        store.start()
        stores.append(store)
    panel_out[...] = panel_row[...].astype(F32)
    for store in stores:
        store.wait()


def finish(meta_all, work, arrived_first, arrived_second, panel_row):
    vmem = pl.BlockSpec(memory_space=pltpu.VMEM)
    return pl.pallas_call(
        finish_kernel,
        out_shape=(
            jax.ShapeDtypeStruct(work.shape, F32), jax.ShapeDtypeStruct((ROWS, PANEL), F32)
        ),
        in_specs=[pl.BlockSpec(memory_space=pltpu.SMEM), vmem, vmem, vmem, vmem],
        out_specs=(pl.BlockSpec(memory_space=pl.ANY), vmem),
        scratch_shapes=[
            pltpu.VMEM(work.shape, F32), pltpu.SemaphoreType.DMA((2,)),
        ],
        compiler_params=pltpu.CompilerParams(vmem_limit_bytes=16 << 20),
        name="finish",
    )(meta_all, work, arrived_first, arrived_second, panel_row)


def shards(child_front, child_inverse, child_index, child_size, front, panel_inverse):
    arrived_first, arrived_second, panel_row, work, meta_all = exchange(
        child_size, child_index, child_front, child_inverse, front, panel_inverse
    )
    return finish(meta_all, work, arrived_first, arrived_second, panel_row)


def solution(mesh):
    in_specs = (
        P("row", "col", None),
        P("row", None, None),
        P("row", None),
        P("row"),
        P("row", "col"),
        P(),
    )
    out_specs = (P("row", "col"), P("row", None))
    return jax.shard_map(shards, mesh=mesh, in_specs=in_specs, out_specs=out_specs, check_vma=False)
```

```python
import functools

import jax
import jax.numpy as jnp
from jax import lax
from jax.experimental import pallas as pl
from jax.experimental.pallas import tpu as pltpu
from jax.sharding import PartitionSpec as P

TILE = 128
PANEL = 256
RUN = 5
SLOTS = 32
PIV = 1024
RUNS = 16
COLS = 8
PART = 512
ROWS = RUN * TILE
PAIR = 2 * TILE
HALF = ROWS // 4
NT = (((1,), (1,)), ((), ()))
NEAR = (1, 3, 4, 12, 5, 15, 7, 13, 2, 8, 9, 6, 11, 14, 10)
BF16 = jnp.bfloat16
F32 = jnp.float32


def tile_rows(index):
    return pl.ds(pl.multiple_of(index * TILE, TILE), TILE)


def slot_table(size_ref, index_ref, index_row, table):
    index_row[...] = jnp.zeros_like(index_row)
    index_row[0:1, 0:SLOTS] = index_ref[...]
    lane = lax.broadcasted_iota(jnp.int32, (1, 128), 1)
    tiles = jnp.where(lane < size_ref[0], index_row[0:1, :], RUN * RUNS)
    tiles = jnp.transpose(jnp.broadcast_to(tiles, (128, 128)))[:SLOTS]
    places = lax.broadcasted_iota(jnp.int32, (SLOTS, 128), 0)

    def total(kept, values):
        return jnp.sum(jnp.where(kept, values, 0), axis=0, keepdims=True)

    one = jnp.ones_like(tiles)
    first = RUN * (lane >> 1)
    order = total(tiles < first, one) + (lane & 1)
    place = jnp.minimum(order, SLOTS - 1)
    local = total(places == place, tiles) - first
    live = (local >= 0) & (local < RUN) & (order < SLOTS)
    same = tiles == lane
    run_first = RUN * ((lane * 205) >> 10)
    held = total(same, one)
    slot = total(same, places) - total(tiles < run_first, one)
    slot = jnp.minimum(jnp.maximum(jnp.where(held > 0, slot, 0), 0), 1)
    for i, values in enumerate((place, jnp.where(live, local, -1), slot, held)):
        table[i:i + 1, :] = values


def exchange_kernel(
    size_ref, index_ref, child_ref, inverse_hbm, front_ref, panel_inverse_ref,
    arrived_first, arrived_second, panel_row, work, meta_all,
    children, factor, column_tiles, outgoing, panel, panel_col, inverse_ref, meta_smem, index_row, meta_vmem,
    own_send, pass_send, sibling_send, gather_recv,
    block_send, block_recv, meta_send, meta_recv, local_sem,
    row_send, row_recv, col_send, col_recv,
):
    arrived = (arrived_first, arrived_second)
    row = lax.axis_index("row")
    col = lax.axis_index("col")
    z, x = row // 4, row % 4
    y, core = col // 2, col % 2
    up = {"row": row, "col": ((y + 1) % 4) * 2 + core}
    down = {"row": row, "col": ((y + 3) % 4) * 2 + core}
    sibling = {"row": row, "col": y * 2 + 1 - core}
    opposite = {"row": row, "col": ((y + 2) % 4) * 2 + core}

    def peer_row(step):
        return ((z + step // 4) % 4) * 4 + (x + step % 4) % 4

    def peer(step):
        return {"row": peer_row(step), "col": col}

    def remote(src, dst, send, recv, device):
        return pltpu.make_async_remote_copy(
            src_ref=src, dst_ref=dst, send_sem=send, recv_sem=recv,
            device_id=device, device_id_type=pl.DeviceIdType.MESH,
        )

    barrier = pltpu.get_barrier_semaphore()
    for device in (up, down, sibling, opposite):
        pl.semaphore_signal(barrier, inc=1, device_id=device, device_id_type=pl.DeviceIdType.MESH)

    @pl.loop(1, RUNS)
    def _(step):
        pl.semaphore_signal(barrier, inc=1, device_id=peer(step), device_id_type=pl.DeviceIdType.MESH)

    inverse_in = pltpu.make_async_copy(inverse_hbm.at[0], inverse_ref, local_sem.at[2])
    inverse_in.start()
    child_in = pltpu.make_async_copy(child_ref.at[0], children.at[pl.ds(col * 4, 4)], local_sem.at[3])
    child_in.start()
    front_in = pltpu.make_async_copy(front_ref, work, local_sem.at[0])
    front_in.start()
    slot_table(size_ref, index_ref, index_row, meta_vmem)
    pl.semaphore_wait(barrier, 4 + RUNS - 1)

    def part_copy(c, t, send, device):
        tile = children.at[c * 4 + t]
        return remote(tile, tile, send, gather_recv.at[c * 4 + t], device)

    below = ((y + 3) % 4) * 2 + core
    above = ((y + 1) % 4) * 2 + core
    across = ((y + 2) % 4) * 2 + core
    sent = []

    def send_part(c, t, send, device, own=False):
        copy = part_copy(c, t, send, device)
        if own:
            copy = remote(
                child_ref.at[0, t], children.at[c * 4 + t], send, gather_recv.at[c * 4 + t], device
            )
        copy.start()
        sent.append(copy)

    def recv_part(c, t):
        part_copy(c, t, own_send.at[0, 0], sibling).wait_recv()

    def make_factor(*tiles):
        rows = jnp.concatenate([children[c * 4 + t] for c, t in tiles], axis=0)
        for j in range(PIV // PAIR):
            depth = (j + 1) * PAIR
            part = lax.dot_general(
                rows[:, :depth], inverse_ref[pl.ds(j * PAIR, PAIR), pl.ds(0, depth)], NT,
                preferred_element_type=F32,
            ).astype(BF16)
            for i, (c, t) in enumerate(tiles):
                factor[c * 4 + t, :, pl.ds(j * PAIR, PAIR)] = part[i * TILE:(i + 1) * TILE]

    up_order, down_order = (0, 1, 2, 3), (2, 3, 0, 1)
    for a, b in zip(up_order, down_order):
        send_part(col, a, own_send.at[0, a], up, own=True)
        send_part(col, b, own_send.at[1, b], down, own=True)
    for t in range(4):
        send_part(col, t, sibling_send.at[0, t], sibling, own=True)

    @pl.loop(1, RUNS)
    def _(step):
        remote(meta_vmem, meta_all.at[row], meta_send.at[step], meta_recv.at[row], peer(step)).start()

    meta_own = pltpu.make_async_copy(meta_vmem, meta_all.at[row], local_sem.at[1])
    meta_own.start()
    child_in.wait()
    inverse_in.wait()
    make_factor((col, 0), (col, 1), (col, 2), (col, 3))
    partner = y * 2 + 1 - core
    for t in range(4):
        recv_part(partner, t)
    make_factor((partner, 0), (partner, 1), (partner, 2), (partner, 3))
    twins = tuple(((y + d) % 4) * 2 + 1 - core for d in (3, 1, 2))
    for a, b in zip(up_order, down_order):
        recv_part(below, a)
        if a < 2:
            send_part(below, a, pass_send.at[0, a], up)
        send_part(below, a, sibling_send.at[1, a], sibling)
        recv_part(above, b)
        if b >= 2:
            send_part(above, b, pass_send.at[1, b - 2], down)
        send_part(above, b, sibling_send.at[2, b], sibling)
        make_factor((below, a), (above, b))
        recv_part(twins[0], a)
        recv_part(twins[1], b)
        make_factor((twins[0], a), (twins[1], b))
    meta_own.wait()

    @pl.loop(1, RUNS)
    def _(step):
        source = peer_row(step)
        remote(
            meta_vmem, meta_all.at[source], meta_send.at[step], meta_recv.at[source], peer(step)
        ).wait_recv()

    meta_in = pltpu.make_async_copy(meta_all, meta_smem, local_sem.at[1])
    meta_in.start()

    for a, b in ((0, 2), (1, 3)):
        for t in (a, b):
            recv_part(across, t)
            send_part(across, t, sibling_send.at[3, t], sibling)
        make_factor((across, a), (across, b))
        for t in (a, b):
            recv_part(twins[2], t)
        make_factor((twins[2], a), (twins[2], b))

    meta_in.wait()

    for slot in range(4):
        column_tiles[pl.ds(slot * TILE, TILE), :] = factor[meta_smem[row, 0, col * 4 + slot]]

    def block(half, target):
        first = factor[meta_smem[row, 0, 2 * target]]
        second = factor[meta_smem[row, 0, 2 * target + 1]]
        rows = jnp.concatenate([first, second], axis=0)
        product = lax.dot_general(
            rows, column_tiles[pl.ds(half * PAIR, PAIR), :], NT, preferred_element_type=F32
        )
        return (-product).astype(BF16)

    def put_block(place, value):
        for a in range(2):
            for b in range(2):
                place[a, b] = value[a * TILE:(a + 1) * TILE, b * TILE:(b + 1) * TILE]

    def block_copy(half, step):
        return remote(
            outgoing.at[half, step], arrived[half].at[row],
            block_send.at[half, step], block_recv.at[half, row], peer(step),
        )

    eager = col != 1
    for half in range(2):
        put_block(arrived[half].at[row], block(half, row))
        held = None
        for step in NEAR:
            put_block(outgoing.at[half, step], block(half, peer_row(step)))
            if held is not None:
                @pl.when(eager)
                def _():
                    block_copy(half, held).start()
            held = step
        @pl.when(eager)
        def _():
            block_copy(half, held).start()

    @pl.when(col == 1)
    def _():
        for half in range(2):
            for step in NEAR:
                block_copy(half, step).start()

    def wait_block(half, step):
        source = peer_row(step)
        remote(
            outgoing.at[half, step], arrived[half].at[source],
            block_send.at[half, step], block_recv.at[half, source], peer(step),
        ).wait_recv()

    def wait_blocks(half):
        @pl.loop(1, RUNS)
        def _(step):
            wait_block(half, step)

    front_in.wait()

    def half_rows(h):
        return pl.ds(h * HALF, HALF)

    def row_copy(h, kind, device):
        return remote(
            panel_row.at[half_rows(h), :], panel_row.at[half_rows(h), :],
            row_send.at[kind, h], row_recv.at[h], device,
        )

    def recv_row(h):
        row_copy(h, 0, sibling).wait_recv()

    wait_blocks(0)

    @pl.when(col == 0)
    def _():
        for j in range(PANEL // TILE):
            @pl.loop(0, RUN)
            def _(i):
                place = (tile_rows(i), pl.ds(j * TILE, TILE))
                total = work[place]
                for child in range(RUNS):
                    tile = arrived_first[
                        child, meta_smem[child, 2, RUN * row + i], meta_smem[child, 2, j]
                    ]
                    here = meta_smem[child, 3, RUN * row + i] * meta_smem[child, 3, j]
                    keep = jnp.full((TILE, TILE), here, jnp.int32) != 0
                    total += jnp.where(keep, tile.astype(F32), 0.0)
                panel[place] = total

        for h in range(4):
            panel_row[half_rows(h), :] = lax.dot_general(
                panel[half_rows(h), :], panel_inverse_ref[...], NT, precision=lax.Precision.HIGHEST,
                preferred_element_type=F32,
            ).astype(BF16)

    kinds = (peer(4), peer(12), peer(8), peer(1), peer(3), peer(2))
    owner_dz = (z + 4 - y) % 4
    mine = (x // 2) == core

    def col_copy(j, h, kind):
        part = panel_col.at[j, half_rows(h), :]
        return remote(part, part, col_send.at[kind, h, j], col_recv.at[j, h], kinds[kind])

    def source_copy(h, kind):
        return remote(
            panel_row.at[half_rows(h), :], panel_col.at[x % 2, half_rows(h), :],
            col_send.at[kind, h, x % 2], col_recv.at[x % 2, h], kinds[kind],
        )

    def recv_col(j, h):
        col_copy(j, h, 0).wait_recv()

    def row_stage(h):
        @pl.when(col == 0)
        def _():
            row_copy(h, 0, up).start()
            row_copy(h, 1, down).start()
            row_copy(h, 2, opposite).start()

        @pl.when((core == 1) | (y > 0))
        def _():
            recv_row(h)

        @pl.when(core == 0)
        def _():
            row_copy(h, 3, sibling).start()

        @pl.when(mine & (owner_dz == 0))
        def _():
            for kind in (2, 0, 1, 5, 3, 4):
                source_copy(h, kind).start()
            panel_col[x % 2, half_rows(h), :] = panel_row[half_rows(h), :]

    def z_stage(h):
        @pl.when(mine & (owner_dz != 0))
        def _():
            recv_col(x % 2, h)
            for kind in (5, 3, 4):
                col_copy(x % 2, h, kind).start()

    for h in range(4):
        row_stage(h)
    for h in range(4):
        z_stage(h)
    for j in (x % 2, 1 - x % 2):
        @pl.when(x != 2 * core + j)
        def _():
            for h in range(4):
                recv_col(j, h)

        span = pl.ds(pl.multiple_of(j * ROWS, TILE), ROWS)
        work[:, span] -= lax.dot_general(
            panel_row[...], panel_col[j], NT, preferred_element_type=F32
        )

    wait_blocks(1)

    for copy in sent:
        copy.wait_send()
    for half in range(2):
        @pl.loop(1, RUNS)
        def _(step):
            block_copy(half, step).wait_send()

    @pl.loop(1, RUNS)
    def _(step):
        remote(meta_vmem, meta_all.at[row], meta_send.at[step], meta_recv.at[row], peer(step)).wait_send()

    for h in range(4):
        @pl.when(core == 0)
        def _():
            row_copy(h, 3, sibling).wait_send()

        @pl.when(col == 0)
        def _():
            row_copy(h, 0, up).wait_send()
            row_copy(h, 1, down).wait_send()
            row_copy(h, 2, opposite).wait_send()

        @pl.when(mine & (owner_dz == 0))
        def _():
            for kind in range(6):
                source_copy(h, kind).wait_send()

        @pl.when(mine & (owner_dz != 0))
        def _():
            for kind in range(3, 6):
                col_copy(x % 2, h, kind).wait_send()


def exchange(child_size, child_index, child_front, child_inverse, front, panel_inverse):
    vmem = pl.BlockSpec(memory_space=pltpu.VMEM)
    dma = pltpu.SemaphoreType.DMA
    return pl.pallas_call(
        exchange_kernel,
        out_shape=(
            pltpu.VMEM((RUNS, 2, 2, TILE, TILE), BF16),
            pltpu.VMEM((RUNS, 2, 2, TILE, TILE), BF16),
            pltpu.VMEM((ROWS, PANEL), BF16),
            pltpu.VMEM(front.shape, F32),
            pltpu.VMEM((RUNS, 4, 128), jnp.int32),
        ),
        in_specs=[
            pl.BlockSpec(memory_space=pltpu.SMEM), vmem, pl.BlockSpec(memory_space=pl.ANY),
            pl.BlockSpec(memory_space=pl.ANY), pl.BlockSpec(memory_space=pl.ANY), vmem,
        ],
        out_specs=(vmem, vmem, vmem, vmem, vmem),
        scratch_shapes=[
            pltpu.VMEM((SLOTS, TILE, PIV), BF16),
            pltpu.VMEM((SLOTS, TILE, PIV), BF16),
            pltpu.VMEM((4 * TILE, PIV), BF16),
            pltpu.VMEM((2, RUNS, 2, 2, TILE, TILE), BF16),
            pltpu.VMEM((ROWS, PANEL), F32),
            pltpu.VMEM((2, ROWS, PANEL), BF16),
            pltpu.VMEM((PIV, PIV), BF16),
            pltpu.SMEM((RUNS, 4, 128), jnp.int32),
            pltpu.VMEM((8, 128), jnp.int32),
            pltpu.VMEM((4, 128), jnp.int32),
            dma((2, 4)), dma((2, 2)), dma((4, 4)), dma((SLOTS,)),
            dma((2, RUNS)), dma((2, RUNS)), dma((RUNS,)), dma((RUNS,)), dma((4,)),
            dma((4, 4)), dma((4,)), dma((6, 4, 2)), dma((2, 4)),
        ],
        compiler_params=pltpu.CompilerParams(
            collective_id=0, has_side_effects=True, vmem_limit_bytes=48 << 20
        ),
        name="exchange",
    )(child_size, child_index, child_front.reshape(1, PART // TILE, TILE, PIV), child_inverse, front, panel_inverse)


def finish_kernel(
    meta_ref, work, arrived_first, arrived_second, panel_row, trailing, panel_out, result, out_sem
):
    row = lax.axis_index("row")
    col = lax.axis_index("col")
    stores = []
    for half, arrived in enumerate((arrived_first, arrived_second)):
        span = pl.ds(half * ROWS, ROWS)
        result[:, span] = work[:, span]

        @pl.loop(0, RUNS)
        def _(child):
            for a in range(2):
                tile_row = meta_ref[child, 1, 2 * row + a]
                for b in range(2):
                    tile_col = meta_ref[child, 1, 4 * col + 2 * half + b]
                    live = (tile_row >= 0) & (tile_col >= 0)
                    keep = jnp.full((TILE, TILE), live.astype(jnp.int32), jnp.int32) != 0
                    place = (
                        tile_rows(jnp.maximum(tile_row, 0)),
                        tile_rows(half * RUN + jnp.maximum(tile_col, 0)),
                    )
                    result[place] += jnp.where(keep, arrived[child, a, b].astype(F32), 0.0)

        store = pltpu.make_async_copy(result.at[:, span], trailing.at[:, span], out_sem.at[half])
        store.start()
        stores.append(store)
    panel_out[...] = panel_row[...].astype(F32)
    for store in stores:
        store.wait()


def finish(meta_all, work, arrived_first, arrived_second, panel_row):
    vmem = pl.BlockSpec(memory_space=pltpu.VMEM)
    return pl.pallas_call(
        finish_kernel,
        out_shape=(
            jax.ShapeDtypeStruct(work.shape, F32), jax.ShapeDtypeStruct((ROWS, PANEL), F32)
        ),
        in_specs=[pl.BlockSpec(memory_space=pltpu.SMEM), vmem, vmem, vmem, vmem],
        out_specs=(pl.BlockSpec(memory_space=pl.ANY), vmem),
        scratch_shapes=[
            pltpu.VMEM(work.shape, F32), pltpu.SemaphoreType.DMA((2,)),
        ],
        compiler_params=pltpu.CompilerParams(vmem_limit_bytes=16 << 20),
        name="finish",
    )(meta_all, work, arrived_first, arrived_second, panel_row)


def shards(child_front, child_inverse, child_index, child_size, front, panel_inverse):
    arrived_first, arrived_second, panel_row, work, meta_all = exchange(
        child_size, child_index, child_front, child_inverse, front, panel_inverse
    )
    return finish(meta_all, work, arrived_first, arrived_second, panel_row)


def solution(mesh):
    in_specs = (
        P("row", "col", None),
        P("row", None, None),
        P("row", None),
        P("row"),
        P("row", "col"),
        P(),
    )
    out_specs = (P("row", "col"), P("row", None))
    return jax.shard_map(shards, mesh=mesh, in_specs=in_specs, out_specs=out_specs, check_vma=False)
```
